128 devices in a mesh: rows: 16 (over x, y), cols: 8 (over z, core).
Axes of the slice: x: 4, y: 4, z: 4, core: 2. Of those that a mesh axis runs over, the one named last changes fastest.
Arguments:
- trace: float32 [32, 8388608], P(None, ('rows', 'cols')), may hold values from -4 to 4
- selectors: int32 [33, 8388608], P(None, ('rows', 'cols')), may hold values 0 or 1
- mds: float32 [32, 32], replicated, may hold values from -1 to 1
- quad: float32 [32], replicated, may hold values from -0.5 to 0.5
- alpha: float32 [33], replicated, may hold values from -1 to 1
- challenges: float32 [2], replicated, may hold values from 0.3 to 0.6
- divisor_inv: float32 [8388608], P(('rows', 'cols')), may hold values from 0.5 to 2
- hash_mds: float32 [12, 12], replicated, may hold values from -6 to 6
- hash_rc: float32 [2, 12], replicated, may hold values from -1 to 1
Outputs:
- digests: float32 [4, 16, 524288], P(None, None, ('rows', 'cols'))
The draws below stay inside these ranges and needn't reach their ends.
All inputs are finite; a program needn't handle non-finite values. No bound on the sum of `selectors` on one device may be relied on, other than what follows from the above.
Results may differ from the reference program's by a relative error of at most 0.00035.
Values sent between devices are 32-bit elements; how exact they have to be, the bound alone decides.
A program may use at most 192 MiB of HBM per device.

```python
import math
import jax
import jax.numpy as jnp
from jax import lax

TRACE_W = 32
CONS = 33
BLOWUP = 8
SEGMENTS = 8
STATE = 12
DIGEST = 4
ROUNDS = 2
LDE = 8388608
N_ROWS = 16


def with_ends(result, key, least, top_value):
    extent = result.shape
    place = [jax.random.randint(jax.random.fold_in(key, axis), (), 0, extent[axis]) for axis in range(len(extent))]
    result = result.at[tuple(place)].set(least)
    longest = extent.index(max(extent))
    place[longest] = (place[longest] + 1) % extent[longest]
    return result.at[tuple(place)].set(top_value)


def level_of(rng, dims, split, least, top_value):
    def one(dim, shards_of):
        steps = jax.random.uniform(jax.random.fold_in(jax.random.fold_in(rng, 6), dim), (shards_of,), jnp.float32, least / len(split), top_value / len(split))
        return jnp.repeat(jnp.exp(steps), dims[dim] // shards_of).reshape((-1,) + (1,) * (len(dims) - dim - 1))

    loudness = one(*split[0])
    for cut in split[1:]:
        loudness = loudness * one(*cut)
    return loudness


def bell_draw(key, extent, deviation, limit, split=(), dtype=jnp.bfloat16):
    array = deviation * jax.random.normal(key, extent, jnp.float32)
    if split:
        array = array * level_of(key, extent, split, -0.22, 0.18)
    return jnp.clip(array, -limit, limit).astype(dtype)


def setup_inputs(seed: int = 0) -> dict:
    splits = jax.random.split(jax.random.key(seed), 10)
    return {
        "trace": bell_draw(splits[0], (TRACE_W, LDE), 1.0, 4.0, ((1, 128),), jnp.float32),
        "selectors": with_ends((jax.random.randint(splits[1], (CONS, LDE), 0, 4) < 3).astype(jnp.int32), jax.random.fold_in(splits[1], 1), 0, 1),
        "mds": bell_draw(splits[2], (TRACE_W, TRACE_W), TRACE_W ** -0.5, 1.0, (), jnp.float32),
        "quad": jnp.clip(jax.random.uniform(splits[3], (TRACE_W,), jnp.float32, -0.5, 0.5), -0.5, 0.5),
        "alpha": bell_draw(splits[4], (CONS,), TRACE_W ** -0.5, 1.0, (), jnp.float32),
        "challenges": jnp.clip(jax.random.uniform(splits[5], (2,), jnp.float32, 0.3, 0.6), 0.3, 0.6),
        "divisor_inv": jnp.clip(jnp.exp(math.log(2.0) - 1.3862944 * jax.random.uniform(splits[6], (LDE,), jnp.float32) ** level_of(splits[6], (LDE,), ((0, 128),), -0.2, 0.2)), 0.5, 2.0),
        "hash_mds": bell_draw(splits[7], (STATE, STATE), 1 ** -0.5, 6.0, (), jnp.float32),
        "hash_rc": jnp.clip(jax.random.uniform(splits[8], (ROUNDS, STATE), jnp.float32, -1.0, 1.0), -1.0, 1.0),
    }


def squash(value):
    return value * lax.rsqrt(1.0 + value * value)

def permute(state, hash_mds, hash_rc):
    for step in range(ROUNDS):
        state = jnp.dot(hash_mds, squash(state), precision=lax.Precision.HIGHEST, preferred_element_type=jnp.float32) + hash_rc[step][:, None]
    return state

def reference(trace, selectors, mds, quad, alpha, challenges, divisor_inv, hash_mds, hash_rc):
    total_rows = trace.shape[1]
    following = jnp.roll(trace, -BLOWUP, axis=1)
    linear = jnp.dot(mds, trace, precision=lax.Precision.HIGHEST, preferred_element_type=jnp.float32)
    cons = following - linear - quad[:, None] * trace * trace
    step_size = challenges[0] / jnp.sqrt(jnp.float32(total_rows))
    gamma = challenges[1]
    numer = 1.0 + step_size * (trace[0] + gamma * trace[1])
    denom = 1.0 + step_size * (trace[2] + gamma * trace[3])
    ratio_log = jnp.log(numer) - jnp.log(denom)
    running = jnp.exp(jnp.cumsum(ratio_log) - ratio_log)
    window = ratio_log
    for offset in range(1, BLOWUP):
        window = window + jnp.roll(ratio_log, -offset)
    grand = running * (jnp.exp(window) * denom - numer) / step_size
    picked = selectors.astype(jnp.float32)
    combined = lax.optimization_barrier(jnp.sum(alpha[:TRACE_W, None] * picked[:TRACE_W] * cons, axis=0)) + alpha[TRACE_W] * picked[TRACE_W] * grand
    quotient = divisor_inv * combined
    spectrum = jnp.fft.fft(quotient) / total_rows
    seg_len = total_rows // SEGMENTS
    real_rows = []
    imag_rows = []
    for segment in range(SEGMENTS):
        piece = spectrum[segment * seg_len:(segment + 1) * seg_len]
        padded = jnp.pad(piece, (0, total_rows - seg_len))
        values = jnp.fft.ifft(padded) * total_rows
        real_rows.append(jnp.real(values).astype(jnp.float32))
        imag_rows.append(jnp.imag(values).astype(jnp.float32))
    real_part = jnp.stack(real_rows)
    imag_part = jnp.stack(imag_rows)
    zeros = jnp.zeros((DIGEST, total_rows), jnp.float32)
    state = permute(jnp.concatenate([zeros, real_part], axis=0), hash_mds, hash_rc)
    state = state + jnp.concatenate([zeros, imag_part], axis=0)
    state = permute(state, hash_mds, hash_rc)
    return state[:DIGEST].reshape(DIGEST, N_ROWS, total_rows // N_ROWS)
```

```python
import math

import jax
import jax.numpy as jnp
from jax import lax
from jax.sharding import PartitionSpec as P

BLOWUP = 8
SEGMENTS = 8
DIGEST = 4
ROUNDS = 2


highest = lax.Precision.HIGHEST


def from_behind(array, axis, by):
    count = lax.axis_size(axis)
    return lax.ppermute(array, axis, [(i, (i + by) % count) for i in range(count)])


def entering(value, axis):
    count, mine = (lax.axis_size(axis), lax.axis_index(axis))
    spread = jnp.broadcast_to(value, (count,))
    pieces = lax.all_to_all(spread, axis, 0, 0, tiled=True)
    earlier = jnp.arange(count, dtype=jnp.int32) < mine
    return jnp.sum(jnp.where(earlier, pieces, jnp.zeros_like(pieces)))


def squash(value):
    return value * lax.rsqrt(1.0 + value * value)


def permute(state, hash_mds, hash_rc):
    for step in range(ROUNDS):
        state = (
            jnp.dot(hash_mds, squash(state), precision=highest, preferred_element_type=jnp.float32)
            + hash_rc[step][:, None]
        )
    return state


def turns(product, modulus, sign):
    angle = sign * 2.0 * math.pi / modulus * (product % modulus).astype(jnp.float32)
    return (jnp.cos(angle), jnp.sin(angle))


def complex_mul(left_re, left_im, right_re, right_im):
    return (left_re * right_re - left_im * right_im, left_re * right_im + left_im * right_re)


def local_dft(values_re, values_im, sign):
    length = values_re.shape[-1]
    first = 128
    second = length // first
    leading = values_re.shape[:-1]
    block_re = values_re.reshape(leading + (first, second))
    block_im = values_im.reshape(leading + (first, second))
    index_one = jnp.arange(first, dtype=jnp.int32)
    index_two = jnp.arange(second, dtype=jnp.int32)
    cos_one, sin_one = turns(index_one[:, None] * index_one[None, :], first, sign)
    section_re = jnp.einsum("kn,...nm->...km", cos_one, block_re, precision=highest) - jnp.einsum(
        "kn,...nm->...km", sin_one, block_im, precision=highest
    )
    section_im = jnp.einsum("kn,...nm->...km", cos_one, block_im, precision=highest) + jnp.einsum(
        "kn,...nm->...km", sin_one, block_re, precision=highest
    )
    twist_cos, twist_sin = turns(index_one[:, None] * index_two[None, :], length, sign)
    section_re, section_im = complex_mul(section_re, section_im, twist_cos, twist_sin)
    cos_two, sin_two = turns(index_two[:, None] * index_two[None, :], second, sign)
    final_re = jnp.einsum("...kn,jn->...kj", section_re, cos_two, precision=highest) - jnp.einsum(
        "...kn,jn->...kj", section_im, sin_two, precision=highest
    )
    final_im = jnp.einsum("...kn,jn->...kj", section_re, sin_two, precision=highest) + jnp.einsum(
        "...kn,jn->...kj", section_im, cos_two, precision=highest
    )
    final_re = jnp.swapaxes(final_re, -1, -2).reshape(leading + (length,))
    final_im = jnp.swapaxes(final_im, -1, -2).reshape(leading + (length,))
    return (final_re, final_im)


def regroup(values):
    return lax.all_to_all(values, ("rows", "cols"), split_axis=1, concat_axis=1, tiled=True)


def column_relay(values):
    return lax.all_to_all(values, "cols", split_axis=1, concat_axis=1, tiled=True)


def on_device(trace, selectors, mds, quad, alpha, challenges, divisor_inv, hash_mds, hash_rc):
    width = trace.shape[0]
    rows_dev = trace.shape[1]
    n_rows = lax.axis_size("rows")
    n_cols = lax.axis_size("cols")
    devices = n_rows * n_cols
    total_rows = rows_dev * devices
    flat_index = lax.axis_index(("rows", "cols"))
    row_index = lax.axis_index("rows")
    rim = from_behind(trace[:, :BLOWUP], ("rows", "cols"), -1)
    extended = jnp.concatenate([trace, rim], axis=1)
    following = extended[:, BLOWUP:]
    linear = jnp.dot(mds, trace, precision=highest, preferred_element_type=jnp.float32)
    cons = following - linear - quad[:, None] * trace * trace
    step_size = challenges[0] / jnp.sqrt(jnp.float32(total_rows))
    gamma = challenges[1]
    numer = 1.0 + step_size * (extended[0] + gamma * extended[1])
    denom = 1.0 + step_size * (extended[2] + gamma * extended[3])
    ratio_log = jnp.log(numer) - jnp.log(denom)
    own_terms = ratio_log[:rows_dev]
    running_sum = jnp.cumsum(own_terms)
    offset = entering(running_sum[-1], ("rows", "cols"))
    running = jnp.exp(offset + running_sum - own_terms)
    window = own_terms
    for shift_step in range(1, BLOWUP):
        window = window + ratio_log[shift_step : shift_step + rows_dev]
    grand = running * (jnp.exp(window) * denom[:rows_dev] - numer[:rows_dev]) / step_size
    picked = selectors.astype(jnp.float32)
    combined = (
        jnp.sum(alpha[:width, None] * picked[:width] * cons, axis=0)
        + alpha[width] * picked[width] * grand
    )
    quotient = divisor_inv * combined
    parts = rows_dev // devices
    gathered = regroup(quotient.reshape(1, rows_dev)).reshape(devices, parts)
    block_index = jnp.arange(devices, dtype=jnp.int32)
    cos_block, sin_block = turns(block_index[:, None] * block_index[None, :], devices, -1.0)
    first_re = jnp.dot(cos_block, gathered, precision=highest, preferred_element_type=jnp.float32)
    first_im = jnp.dot(sin_block, gathered, precision=highest, preferred_element_type=jnp.float32)
    global_pos = flat_index * parts + jnp.arange(parts, dtype=jnp.int32)
    twist_cos, twist_sin = turns(block_index[:, None] * global_pos[None, :], total_rows, -1.0)
    first_re, first_im = complex_mul(first_re, first_im, twist_cos, twist_sin)
    ordered = (
        jnp.stack([first_re, first_im])
        .reshape(2, n_cols, n_rows, parts)
        .transpose(0, 2, 1, 3)
        .reshape(2, devices * parts)
    )
    columns = regroup(ordered)
    coef_re, coef_im = local_dft(columns[0], columns[1], -1.0)
    coef_re = coef_re / total_rows
    coef_im = coef_im / total_rows
    seg_dev = SEGMENTS // n_cols
    seg_rows = rows_dev // SEGMENTS
    packed = jnp.stack([coef_re, coef_im]).reshape(2, n_cols, seg_dev, seg_rows)
    owned = column_relay(packed)
    owned = owned.transpose(0, 2, 3, 1).reshape(2, seg_dev, seg_rows * n_cols)
    short = seg_rows * n_cols
    band = short * SEGMENTS
    phase_index = jnp.arange(SEGMENTS, dtype=jnp.int32)
    short_index = jnp.arange(short, dtype=jnp.int32)
    phase_cos, phase_sin = turns(phase_index[:, None] * short_index[None, :], band, 1.0)
    spread_re, spread_im = complex_mul(
        owned[0][:, None, :], owned[1][:, None, :], phase_cos, phase_sin
    )
    lift_re, lift_im = local_dft(spread_re, spread_im, 1.0)
    lift_re = jnp.swapaxes(lift_re, 1, 2).reshape(seg_dev, band)
    lift_im = jnp.swapaxes(lift_im, 1, 2).reshape(seg_dev, band)
    band_index = jnp.arange(band, dtype=jnp.int32)
    shift_cos, shift_sin = turns(band_index * row_index, total_rows, 1.0)
    lift_re, lift_im = complex_mul(lift_re, lift_im, shift_cos, shift_sin)
    lifted = jnp.stack([lift_re, lift_im])
    slab = band // n_rows
    small = band // devices
    row_ids = jnp.arange(n_rows, dtype=jnp.int32)
    cos_rows, sin_rows = turns(row_ids[:, None] * row_ids[None, :], n_rows, 1.0)
    pieces = lifted.reshape(2, seg_dev, n_rows, slab).transpose(0, 2, 1, 3)
    arrived = lax.all_to_all(pieces, "rows", split_axis=1, concat_axis=1, tiled=True)
    summed_re = jnp.einsum("ab,b...->a...", cos_rows, arrived[0], precision=highest) - jnp.einsum(
        "ab,b...->a...", sin_rows, arrived[1], precision=highest
    )
    summed_im = jnp.einsum("ab,b...->a...", sin_rows, arrived[0], precision=highest) + jnp.einsum(
        "ab,b...->a...", cos_rows, arrived[1], precision=highest
    )
    outgoing = (
        jnp.stack([summed_re, summed_im])
        .reshape(2, n_rows, seg_dev, n_cols, small)
        .transpose(0, 3, 2, 1, 4)
    )
    landed = column_relay(outgoing)
    values = landed.reshape(2, SEGMENTS, n_rows, small)
    leaf_count = n_rows * small
    real_part = values[0].reshape(SEGMENTS, leaf_count)
    imag_part = values[1].reshape(SEGMENTS, leaf_count)
    zeros = jnp.zeros((DIGEST, leaf_count), jnp.float32)
    state = permute(jnp.concatenate([zeros, real_part], axis=0), hash_mds, hash_rc)
    state = state + jnp.concatenate([zeros, imag_part], axis=0)
    state = permute(state, hash_mds, hash_rc)
    return state[:DIGEST].reshape(DIGEST, n_rows, small)


def solution(mesh):
    in_specs = (
        P(None, ("rows", "cols")),
        P(None, ("rows", "cols")),
        P(),
        P(),
        P(),
        P(),
        P(("rows", "cols")),
        P(),
        P(),
    )
    out_specs = P(None, None, ("rows", "cols"))
    return jax.shard_map(
        on_device, mesh=mesh, in_specs=in_specs, out_specs=out_specs, check_vma=False
    )
```

```python
import math

import jax
import jax.numpy as jnp
from jax import lax
from jax.sharding import PartitionSpec as P

BLOWUP = 8
SEGMENTS = 8
DIGEST = 4
ROUNDS = 2


highest = lax.Precision.HIGHEST


def from_behind(array, axis, by):
    count = lax.axis_size(axis)
    return lax.ppermute(array, axis, [(i, (i + by) % count) for i in range(count)])


def entering(value, axis):
    count, mine = (lax.axis_size(axis), lax.axis_index(axis))
    spread = jnp.broadcast_to(value, (count,))
    pieces = lax.all_to_all(spread, axis, 0, 0, tiled=True)
    earlier = jnp.arange(count, dtype=jnp.int32) < mine
    return jnp.sum(jnp.where(earlier, pieces, jnp.zeros_like(pieces)))


def squash(value):
    return value * lax.rsqrt(1.0 + value * value)


def permute(state, hash_mds, hash_rc):
    for step in range(ROUNDS):
        state = (
            jnp.dot(hash_mds, squash(state), precision=highest, preferred_element_type=jnp.float32)
            + hash_rc[step][:, None]
        )
    return state


def turns(product, modulus, sign):
    angle = sign * 2.0 * math.pi / modulus * (product % modulus).astype(jnp.float32)
    return (jnp.cos(angle), jnp.sin(angle))


def complex_mul(left_re, left_im, right_re, right_im):
    return (left_re * right_re - left_im * right_im, left_re * right_im + left_im * right_re)


def local_dft(values_re, values_im, sign):
    length = values_re.shape[-1]
    first = 128
    second = length // first
    leading = values_re.shape[:-1]
    block_re = values_re.reshape(leading + (first, second))
    block_im = values_im.reshape(leading + (first, second))
    index_one = jnp.arange(first, dtype=jnp.int32)
    index_two = jnp.arange(second, dtype=jnp.int32)
    cos_one, sin_one = turns(index_one[:, None] * index_one[None, :], first, sign)
    section_re = jnp.einsum("kn,...nm->...km", cos_one, block_re, precision=highest) - jnp.einsum(
        "kn,...nm->...km", sin_one, block_im, precision=highest
    )
    section_im = jnp.einsum("kn,...nm->...km", cos_one, block_im, precision=highest) + jnp.einsum(
        "kn,...nm->...km", sin_one, block_re, precision=highest
    )
    twist_cos, twist_sin = turns(index_one[:, None] * index_two[None, :], length, sign)
    section_re, section_im = complex_mul(section_re, section_im, twist_cos, twist_sin)
    cos_two, sin_two = turns(index_two[:, None] * index_two[None, :], second, sign)
    final_re = jnp.einsum("...kn,jn->...kj", section_re, cos_two, precision=highest) - jnp.einsum(
        "...kn,jn->...kj", section_im, sin_two, precision=highest
    )
    final_im = jnp.einsum("...kn,jn->...kj", section_re, sin_two, precision=highest) + jnp.einsum(
        "...kn,jn->...kj", section_im, cos_two, precision=highest
    )
    final_re = jnp.swapaxes(final_re, -1, -2).reshape(leading + (length,))
    final_im = jnp.swapaxes(final_im, -1, -2).reshape(leading + (length,))
    return (final_re, final_im)


def lift_dft(values_re, values_im, sign):
    segs, phases, length = values_re.shape
    first = 128
    second = length // first
    block_re = values_re.reshape(segs, phases, first, second)
    block_im = values_im.reshape(segs, phases, first, second)
    index_one = jnp.arange(first, dtype=jnp.int32)
    index_two = jnp.arange(second, dtype=jnp.int32)
    cos_one, sin_one = turns(index_one[:, None] * index_one[None, :], first, sign)
    section_re = jnp.einsum("kn,spnm->skpm", cos_one, block_re, precision=highest) - jnp.einsum(
        "kn,spnm->skpm", sin_one, block_im, precision=highest
    )
    section_im = jnp.einsum("kn,spnm->skpm", cos_one, block_im, precision=highest) + jnp.einsum(
        "kn,spnm->skpm", sin_one, block_re, precision=highest
    )
    twist_cos, twist_sin = turns(index_one[:, None] * index_two[None, :], length, sign)
    section_re, section_im = complex_mul(
        section_re, section_im, twist_cos[:, None, :], twist_sin[:, None, :]
    )
    section_re = section_re.reshape(segs, first * phases, second)
    section_im = section_im.reshape(segs, first * phases, second)
    cos_two, sin_two = turns(index_two[:, None] * index_two[None, :], second, sign)
    final_re = jnp.einsum("jm,sxm->sjx", cos_two, section_re, precision=highest) - jnp.einsum(
        "jm,sxm->sjx", sin_two, section_im, precision=highest
    )
    final_im = jnp.einsum("jm,sxm->sjx", sin_two, section_re, precision=highest) + jnp.einsum(
        "jm,sxm->sjx", cos_two, section_im, precision=highest
    )
    return (final_re.reshape(segs, length * phases), final_im.reshape(segs, length * phases))


def regroup(values):
    return lax.all_to_all(values, ("rows", "cols"), split_axis=1, concat_axis=1, tiled=True)


def column_relay(values):
    return lax.all_to_all(values, "cols", split_axis=1, concat_axis=1, tiled=True)


def on_device(trace, selectors, mds, quad, alpha, challenges, divisor_inv, hash_mds, hash_rc):
    width = trace.shape[0]
    rows_dev = trace.shape[1]
    n_rows = lax.axis_size("rows")
    n_cols = lax.axis_size("cols")
    devices = n_rows * n_cols
    total_rows = rows_dev * devices
    flat_index = lax.axis_index(("rows", "cols"))
    row_index = lax.axis_index("rows")
    rim = from_behind(trace[:, :BLOWUP], ("rows", "cols"), -1)
    extended = jnp.concatenate([trace, rim], axis=1)
    following = extended[:, BLOWUP:]
    linear = jnp.dot(mds, trace, precision=highest, preferred_element_type=jnp.float32)
    cons = following - linear - quad[:, None] * trace * trace
    step_size = challenges[0] / jnp.sqrt(jnp.float32(total_rows))
    gamma = challenges[1]
    numer = 1.0 + step_size * (extended[0] + gamma * extended[1])
    denom = 1.0 + step_size * (extended[2] + gamma * extended[3])
    ratio_log = jnp.log(numer) - jnp.log(denom)
    own_terms = ratio_log[:rows_dev]
    running_sum = jnp.cumsum(own_terms)
    offset = entering(running_sum[-1], ("rows", "cols"))
    running = jnp.exp(offset + running_sum - own_terms)
    window = own_terms
    for shift_step in range(1, BLOWUP):
        window = window + ratio_log[shift_step : shift_step + rows_dev]
    grand = running * (jnp.exp(window) * denom[:rows_dev] - numer[:rows_dev]) / step_size
    picked = selectors.astype(jnp.float32)
    combined = (
        jnp.sum(alpha[:width, None] * picked[:width] * cons, axis=0)
        + alpha[width] * picked[width] * grand
    )
    quotient = divisor_inv * combined
    parts = rows_dev // devices
    gathered = regroup(quotient.reshape(1, rows_dev)).reshape(devices, parts)
    block_index = jnp.arange(devices, dtype=jnp.int32)
    cos_block, sin_block = turns(block_index[:, None] * block_index[None, :], devices, -1.0)
    first_re = jnp.dot(cos_block, gathered, precision=highest, preferred_element_type=jnp.float32)
    first_im = jnp.dot(sin_block, gathered, precision=highest, preferred_element_type=jnp.float32)
    global_pos = flat_index * parts + jnp.arange(parts, dtype=jnp.int32)
    twist_cos, twist_sin = turns(block_index[:, None] * global_pos[None, :], total_rows, -1.0)
    first_re, first_im = complex_mul(first_re, first_im, twist_cos, twist_sin)
    ordered = (
        jnp.stack([first_re, first_im])
        .reshape(2, n_cols, n_rows, parts)
        .transpose(0, 2, 1, 3)
        .reshape(2, devices * parts)
    )
    columns = regroup(ordered)
    coef_re, coef_im = local_dft(columns[0], columns[1], -1.0)
    coef_re = coef_re / total_rows
    coef_im = coef_im / total_rows
    seg_dev = SEGMENTS // n_cols
    seg_rows = rows_dev // SEGMENTS
    packed = jnp.stack([coef_re, coef_im]).reshape(2, n_cols, seg_dev, seg_rows)
    owned = column_relay(packed)
    owned = owned.transpose(0, 2, 3, 1).reshape(2, seg_dev, seg_rows * n_cols)
    short = seg_rows * n_cols
    band = short * SEGMENTS
    phase_index = jnp.arange(SEGMENTS, dtype=jnp.int32)
    short_index = jnp.arange(short, dtype=jnp.int32)
    phase_cos, phase_sin = turns(phase_index[:, None] * short_index[None, :], band, 1.0)
    spread_re, spread_im = complex_mul(
        owned[0][:, None, :], owned[1][:, None, :], phase_cos, phase_sin
    )
    lift_re, lift_im = lift_dft(spread_re, spread_im, 1.0)
    band_index = jnp.arange(band, dtype=jnp.int32)
    shift_cos, shift_sin = turns(band_index * row_index, total_rows, 1.0)
    lift_re, lift_im = complex_mul(lift_re, lift_im, shift_cos, shift_sin)
    lifted = jnp.stack([lift_re, lift_im])
    slab = band // n_rows
    small = band // devices
    row_ids = jnp.arange(n_rows, dtype=jnp.int32)
    cos_rows, sin_rows = turns(row_ids[:, None] * row_ids[None, :], n_rows, 1.0)
    pieces = lifted.reshape(2, seg_dev, n_rows, slab).transpose(0, 2, 1, 3)
    arrived = lax.all_to_all(pieces, "rows", split_axis=1, concat_axis=1, tiled=True)
    summed_re = jnp.einsum("ab,b...->a...", cos_rows, arrived[0], precision=highest) - jnp.einsum(
        "ab,b...->a...", sin_rows, arrived[1], precision=highest
    )
    summed_im = jnp.einsum("ab,b...->a...", sin_rows, arrived[0], precision=highest) + jnp.einsum(
        "ab,b...->a...", cos_rows, arrived[1], precision=highest
    )
    outgoing = (
        jnp.stack([summed_re, summed_im])
        .reshape(2, n_rows, seg_dev, n_cols, small)
        .transpose(0, 3, 2, 1, 4)
    )
    landed = column_relay(outgoing)
    values = landed.reshape(2, SEGMENTS, n_rows, small)
    leaf_count = n_rows * small
    real_part = values[0].reshape(SEGMENTS, leaf_count)
    imag_part = values[1].reshape(SEGMENTS, leaf_count)
    zeros = jnp.zeros((DIGEST, leaf_count), jnp.float32)
    state = permute(jnp.concatenate([zeros, real_part], axis=0), hash_mds, hash_rc)
    state = state + jnp.concatenate([zeros, imag_part], axis=0)
    state = permute(state, hash_mds, hash_rc)
    return state[:DIGEST].reshape(DIGEST, n_rows, small)


def solution(mesh):
    in_specs = (
        P(None, ("rows", "cols")),
        P(None, ("rows", "cols")),
        P(),
        P(),
        P(),
        P(),
        P(("rows", "cols")),
        P(),
        P(),
    )
    out_specs = P(None, None, ("rows", "cols"))
    return jax.shard_map(
        on_device, mesh=mesh, in_specs=in_specs, out_specs=out_specs, check_vma=False
    )
```

```python
import math

import jax
import jax.numpy as jnp
from jax import lax
from jax.sharding import PartitionSpec as P

BLOWUP = 8
SEGMENTS = 8
DIGEST = 4
ROUNDS = 2


highest = lax.Precision.HIGHEST


def from_behind(array, axis, by):
    count = lax.axis_size(axis)
    return lax.ppermute(array, axis, [(i, (i + by) % count) for i in range(count)])


def entering(value, axis):
    count, mine = (lax.axis_size(axis), lax.axis_index(axis))
    spread = jnp.broadcast_to(value, (count,))
    pieces = lax.all_to_all(spread, axis, 0, 0, tiled=True)
    earlier = jnp.arange(count, dtype=jnp.int32) < mine
    return jnp.sum(jnp.where(earlier, pieces, jnp.zeros_like(pieces)))


def squash(value):
    return value * lax.rsqrt(1.0 + value * value)


def permute(state, hash_mds, hash_rc):
    for step in range(ROUNDS):
        state = (
            jnp.dot(hash_mds, squash(state), precision=highest, preferred_element_type=jnp.float32)
            + hash_rc[step][:, None]
        )
    return state


def turns(product, modulus, sign):
    angle = sign * 2.0 * math.pi / modulus * (product % modulus).astype(jnp.float32)
    return (jnp.cos(angle), jnp.sin(angle))


def complex_mul(left_re, left_im, right_re, right_im):
    return (left_re * right_re - left_im * right_im, left_re * right_im + left_im * right_re)


def local_dft(values_re, values_im, sign):
    length = values_re.shape[-1]
    first = 128
    second = length // first
    leading = values_re.shape[:-1]
    block_re = values_re.reshape(leading + (first, second))
    block_im = values_im.reshape(leading + (first, second))
    index_one = jnp.arange(first, dtype=jnp.int32)
    index_two = jnp.arange(second, dtype=jnp.int32)
    cos_one, sin_one = turns(index_one[:, None] * index_one[None, :], first, sign)
    section_re = jnp.einsum("kn,...nm->...km", cos_one, block_re, precision=highest) - jnp.einsum(
        "kn,...nm->...km", sin_one, block_im, precision=highest
    )
    section_im = jnp.einsum("kn,...nm->...km", cos_one, block_im, precision=highest) + jnp.einsum(
        "kn,...nm->...km", sin_one, block_re, precision=highest
    )
    twist_cos, twist_sin = turns(index_one[:, None] * index_two[None, :], length, sign)
    section_re, section_im = complex_mul(section_re, section_im, twist_cos, twist_sin)
    cos_two, sin_two = turns(index_two[:, None] * index_two[None, :], second, sign)
    final_re = jnp.einsum("...kn,jn->...kj", section_re, cos_two, precision=highest) - jnp.einsum(
        "...kn,jn->...kj", section_im, sin_two, precision=highest
    )
    final_im = jnp.einsum("...kn,jn->...kj", section_re, sin_two, precision=highest) + jnp.einsum(
        "...kn,jn->...kj", section_im, cos_two, precision=highest
    )
    final_re = jnp.swapaxes(final_re, -1, -2).reshape(leading + (length,))
    final_im = jnp.swapaxes(final_im, -1, -2).reshape(leading + (length,))
    return (final_re, final_im)


def lift_dft(values_re, values_im, sign):
    segs, phases, length = values_re.shape
    first = 128
    second = length // first
    block_re = values_re.reshape(segs, phases, first, second)
    block_im = values_im.reshape(segs, phases, first, second)
    index_one = jnp.arange(first, dtype=jnp.int32)
    index_two = jnp.arange(second, dtype=jnp.int32)
    cos_one, sin_one = turns(index_one[:, None] * index_one[None, :], first, sign)
    section_re = jnp.einsum("kn,spnm->skpm", cos_one, block_re, precision=highest) - jnp.einsum(
        "kn,spnm->skpm", sin_one, block_im, precision=highest
    )
    section_im = jnp.einsum("kn,spnm->skpm", cos_one, block_im, precision=highest) + jnp.einsum(
        "kn,spnm->skpm", sin_one, block_re, precision=highest
    )
    twist_cos, twist_sin = turns(index_one[:, None] * index_two[None, :], length, sign)
    section_re, section_im = complex_mul(
        section_re, section_im, twist_cos[:, None, :], twist_sin[:, None, :]
    )
    section_re = section_re.reshape(segs, first * phases, second)
    section_im = section_im.reshape(segs, first * phases, second)
    cos_two, sin_two = turns(index_two[:, None] * index_two[None, :], second, sign)
    final_re = jnp.einsum("jm,sxm->sjx", cos_two, section_re, precision=highest) - jnp.einsum(
        "jm,sxm->sjx", sin_two, section_im, precision=highest
    )
    final_im = jnp.einsum("jm,sxm->sjx", sin_two, section_re, precision=highest) + jnp.einsum(
        "jm,sxm->sjx", cos_two, section_im, precision=highest
    )
    return (final_re.reshape(segs, length * phases), final_im.reshape(segs, length * phases))


def regroup(values):
    return lax.all_to_all(values, ("rows", "cols"), split_axis=1, concat_axis=1, tiled=True)


def column_relay(values):
    return lax.all_to_all(values, "cols", split_axis=1, concat_axis=1, tiled=True)


def on_device(trace, selectors, mds, quad, alpha, challenges, divisor_inv, hash_mds, hash_rc):
    width = trace.shape[0]
    rows_dev = trace.shape[1]
    n_rows = lax.axis_size("rows")
    n_cols = lax.axis_size("cols")
    devices = n_rows * n_cols
    total_rows = rows_dev * devices
    flat_index = lax.axis_index(("rows", "cols"))
    row_index = lax.axis_index("rows")
    rim = from_behind(trace[:, :BLOWUP], ("rows", "cols"), -1)
    extended = jnp.concatenate([trace, rim], axis=1)
    following = extended[:, BLOWUP:]
    linear = jnp.dot(mds, trace, precision=highest, preferred_element_type=jnp.float32)
    cons = following - linear - quad[:, None] * trace * trace
    step_size = challenges[0] / jnp.sqrt(jnp.float32(total_rows))
    gamma = challenges[1]
    numer = 1.0 + step_size * (extended[0] + gamma * extended[1])
    denom = 1.0 + step_size * (extended[2] + gamma * extended[3])
    ratio_log = jnp.log(numer) - jnp.log(denom)
    own_terms = ratio_log[:rows_dev]
    running_sum = jnp.cumsum(own_terms)
    offset = entering(running_sum[-1], ("rows", "cols"))
    running = jnp.exp(offset + running_sum - own_terms)
    window = own_terms
    for shift_step in range(1, BLOWUP):
        window = window + ratio_log[shift_step : shift_step + rows_dev]
    grand = running * (jnp.exp(window) * denom[:rows_dev] - numer[:rows_dev]) / step_size
    picked = selectors.astype(jnp.float32)
    combined = (
        jnp.sum(alpha[:width, None] * picked[:width] * cons, axis=0)
        + alpha[width] * picked[width] * grand
    )
    quotient = divisor_inv * combined
    parts = rows_dev // devices
    gathered = regroup(quotient.reshape(1, rows_dev)).reshape(devices, parts)
    block_index = jnp.arange(devices, dtype=jnp.int32)
    cos_block, sin_block = turns(block_index[:, None] * block_index[None, :], devices, -1.0)
    first_re = jnp.dot(cos_block, gathered, precision=highest, preferred_element_type=jnp.float32)
    first_im = jnp.dot(sin_block, gathered, precision=highest, preferred_element_type=jnp.float32)
    global_pos = flat_index * parts + jnp.arange(parts, dtype=jnp.int32)
    twist_cos, twist_sin = turns(block_index[:, None] * global_pos[None, :], total_rows, -1.0)
    first_re, first_im = complex_mul(first_re, first_im, twist_cos, twist_sin)
    ordered = (
        jnp.stack([first_re, first_im])
        .reshape(2, n_cols, n_rows, parts)
        .transpose(0, 2, 1, 3)
        .reshape(2, devices * parts)
    )
    columns = regroup(ordered)
    coef_re, coef_im = local_dft(columns[0], columns[1], -1.0)
    coef_re = coef_re / total_rows
    coef_im = coef_im / total_rows
    seg_dev = SEGMENTS // n_cols
    seg_rows = rows_dev // SEGMENTS
    packed = jnp.stack([coef_re, coef_im]).reshape(2, n_cols, seg_dev, seg_rows)
    owned = column_relay(packed)
    owned = owned.transpose(0, 2, 3, 1).reshape(2, seg_dev, seg_rows * n_cols)
    short = seg_rows * n_cols
    band = short * SEGMENTS
    phase_index = jnp.arange(SEGMENTS, dtype=jnp.int32)
    short_index = jnp.arange(short, dtype=jnp.int32)
    phase_cos, phase_sin = turns(phase_index[:, None] * short_index[None, :], band, 1.0)
    spread_re, spread_im = complex_mul(
        owned[0][:, None, :], owned[1][:, None, :], phase_cos, phase_sin
    )
    lift_re, lift_im = lift_dft(spread_re, spread_im, 1.0)
    band_index = jnp.arange(band, dtype=jnp.int32)
    shift_cos, shift_sin = turns(band_index * row_index, total_rows, 1.0)
    lift_re, lift_im = complex_mul(lift_re, lift_im, shift_cos, shift_sin)
    small = band // devices
    lifted = (
        jnp.stack([lift_re, lift_im])
        .reshape(2, seg_dev, devices, small)
        .transpose(0, 2, 1, 3)
    )
    arrived = regroup(lifted).reshape(2, n_rows, n_cols, seg_dev, small)
    row_ids = jnp.arange(n_rows, dtype=jnp.int32)
    cos_rows, sin_rows = turns(row_ids[:, None] * row_ids[None, :], n_rows, 1.0)
    summed_re = jnp.einsum("ab,bcsu->csau", cos_rows, arrived[0], precision=highest) - jnp.einsum(
        "ab,bcsu->csau", sin_rows, arrived[1], precision=highest
    )
    summed_im = jnp.einsum("ab,bcsu->csau", sin_rows, arrived[0], precision=highest) + jnp.einsum(
        "ab,bcsu->csau", cos_rows, arrived[1], precision=highest
    )
    values = jnp.stack([summed_re, summed_im]).reshape(2, SEGMENTS, n_rows, small)
    leaf_count = n_rows * small
    real_part = values[0].reshape(SEGMENTS, leaf_count)
    imag_part = values[1].reshape(SEGMENTS, leaf_count)
    zeros = jnp.zeros((DIGEST, leaf_count), jnp.float32)
    state = permute(jnp.concatenate([zeros, real_part], axis=0), hash_mds, hash_rc)
    state = state + jnp.concatenate([zeros, imag_part], axis=0)
    state = permute(state, hash_mds, hash_rc)
    return state[:DIGEST].reshape(DIGEST, n_rows, small)


def solution(mesh):
    in_specs = (
        P(None, ("rows", "cols")),
        P(None, ("rows", "cols")),
        P(),
        P(),
        P(),
        P(),
        P(("rows", "cols")),
        P(),
        P(),
    )
    out_specs = P(None, None, ("rows", "cols"))
    return jax.shard_map(
        on_device, mesh=mesh, in_specs=in_specs, out_specs=out_specs, check_vma=False
    )
```

```python
import math

import jax
import jax.numpy as jnp
from jax import lax
from jax.sharding import PartitionSpec as P

BLOWUP = 8
SEGMENTS = 8
DIGEST = 4
ROUNDS = 2


highest = lax.Precision.HIGHEST
three_pass = lax.Precision.HIGH


def from_behind(array, axis, by):
    count = lax.axis_size(axis)
    return lax.ppermute(array, axis, [(i, (i + by) % count) for i in range(count)])


def entering(value, axis):
    count, mine = (lax.axis_size(axis), lax.axis_index(axis))
    spread = jnp.broadcast_to(value, (count,))
    pieces = lax.all_to_all(spread, axis, 0, 0, tiled=True)
    earlier = jnp.arange(count, dtype=jnp.int32) < mine
    return jnp.sum(jnp.where(earlier, pieces, jnp.zeros_like(pieces)))


def squash(value):
    return value * lax.rsqrt(1.0 + value * value)


def permute(state, hash_mds, hash_rc):
    for step in range(ROUNDS):
        state = (
            jnp.dot(hash_mds, squash(state), precision=highest, preferred_element_type=jnp.float32)
            + hash_rc[step][:, None]
        )
    return state


def turns(product, modulus, sign):
    angle = sign * 2.0 * math.pi / modulus * (product % modulus).astype(jnp.float32)
    return (jnp.cos(angle), jnp.sin(angle))


def complex_mul(left_re, left_im, right_re, right_im):
    return (left_re * right_re - left_im * right_im, left_re * right_im + left_im * right_re)


def local_dft(values_re, values_im, sign):
    length = values_re.shape[-1]
    first = 128
    second = length // first
    leading = values_re.shape[:-1]
    block_re = values_re.reshape(leading + (first, second))
    block_im = values_im.reshape(leading + (first, second))
    index_one = jnp.arange(first, dtype=jnp.int32)
    index_two = jnp.arange(second, dtype=jnp.int32)
    cos_one, sin_one = turns(index_one[:, None] * index_one[None, :], first, sign)
    section_re = jnp.einsum("kn,...nm->...km", cos_one, block_re, precision=three_pass) - jnp.einsum(
        "kn,...nm->...km", sin_one, block_im, precision=three_pass
    )
    section_im = jnp.einsum("kn,...nm->...km", cos_one, block_im, precision=three_pass) + jnp.einsum(
        "kn,...nm->...km", sin_one, block_re, precision=three_pass
    )
    twist_cos, twist_sin = turns(index_one[:, None] * index_two[None, :], length, sign)
    section_re, section_im = complex_mul(section_re, section_im, twist_cos, twist_sin)
    cos_two, sin_two = turns(index_two[:, None] * index_two[None, :], second, sign)
    final_re = jnp.einsum("...kn,jn->...kj", section_re, cos_two, precision=three_pass) - jnp.einsum(
        "...kn,jn->...kj", section_im, sin_two, precision=three_pass
    )
    final_im = jnp.einsum("...kn,jn->...kj", section_re, sin_two, precision=three_pass) + jnp.einsum(
        "...kn,jn->...kj", section_im, cos_two, precision=three_pass
    )
    final_re = jnp.swapaxes(final_re, -1, -2).reshape(leading + (length,))
    final_im = jnp.swapaxes(final_im, -1, -2).reshape(leading + (length,))
    return (final_re, final_im)


def lift_dft(values_re, values_im, sign):
    segs, phases, length = values_re.shape
    first = 128
    second = length // first
    block_re = values_re.reshape(segs, phases, first, second)
    block_im = values_im.reshape(segs, phases, first, second)
    index_one = jnp.arange(first, dtype=jnp.int32)
    index_two = jnp.arange(second, dtype=jnp.int32)
    cos_one, sin_one = turns(index_one[:, None] * index_one[None, :], first, sign)
    section_re = jnp.einsum("kn,spnm->skpm", cos_one, block_re, precision=three_pass) - jnp.einsum(
        "kn,spnm->skpm", sin_one, block_im, precision=three_pass
    )
    section_im = jnp.einsum("kn,spnm->skpm", cos_one, block_im, precision=three_pass) + jnp.einsum(
        "kn,spnm->skpm", sin_one, block_re, precision=three_pass
    )
    twist_cos, twist_sin = turns(index_one[:, None] * index_two[None, :], length, sign)
    section_re, section_im = complex_mul(
        section_re, section_im, twist_cos[:, None, :], twist_sin[:, None, :]
    )
    section_re = section_re.reshape(segs, first * phases, second)
    section_im = section_im.reshape(segs, first * phases, second)
    cos_two, sin_two = turns(index_two[:, None] * index_two[None, :], second, sign)
    final_re = jnp.einsum("jm,sxm->sjx", cos_two, section_re, precision=three_pass) - jnp.einsum(
        "jm,sxm->sjx", sin_two, section_im, precision=three_pass
    )
    final_im = jnp.einsum("jm,sxm->sjx", sin_two, section_re, precision=three_pass) + jnp.einsum(
        "jm,sxm->sjx", cos_two, section_im, precision=three_pass
    )
    return (final_re.reshape(segs, length * phases), final_im.reshape(segs, length * phases))


def regroup(values):
    return lax.all_to_all(values, ("rows", "cols"), split_axis=1, concat_axis=1, tiled=True)


def column_relay(values):
    return lax.all_to_all(values, "cols", split_axis=1, concat_axis=1, tiled=True)


def on_device(trace, selectors, mds, quad, alpha, challenges, divisor_inv, hash_mds, hash_rc):
    width = trace.shape[0]
    rows_dev = trace.shape[1]
    n_rows = lax.axis_size("rows")
    n_cols = lax.axis_size("cols")
    devices = n_rows * n_cols
    total_rows = rows_dev * devices
    flat_index = lax.axis_index(("rows", "cols"))
    row_index = lax.axis_index("rows")
    rim = from_behind(trace[:, :BLOWUP], ("rows", "cols"), -1)
    extended = jnp.concatenate([trace, rim], axis=1)
    following = extended[:, BLOWUP:]
    linear = jnp.dot(mds, trace, precision=highest, preferred_element_type=jnp.float32)
    cons = following - linear - quad[:, None] * trace * trace
    step_size = challenges[0] / jnp.sqrt(jnp.float32(total_rows))
    gamma = challenges[1]
    numer = 1.0 + step_size * (extended[0] + gamma * extended[1])
    denom = 1.0 + step_size * (extended[2] + gamma * extended[3])
    ratio_log = jnp.log(numer) - jnp.log(denom)
    own_terms = ratio_log[:rows_dev]
    running_sum = jnp.cumsum(own_terms)
    offset = entering(running_sum[-1], ("rows", "cols"))
    running = jnp.exp(offset + running_sum - own_terms)
    window = own_terms
    for shift_step in range(1, BLOWUP):
        window = window + ratio_log[shift_step : shift_step + rows_dev]
    grand = running * (jnp.exp(window) * denom[:rows_dev] - numer[:rows_dev]) / step_size
    picked = selectors.astype(jnp.float32)
    combined = (
        jnp.sum(alpha[:width, None] * picked[:width] * cons, axis=0)
        + alpha[width] * picked[width] * grand
    )
    quotient = divisor_inv * combined
    parts = rows_dev // devices
    gathered = regroup(quotient.reshape(1, rows_dev)).reshape(devices, parts)
    block_index = jnp.arange(devices, dtype=jnp.int32)
    cos_block, sin_block = turns(block_index[:, None] * block_index[None, :], devices, -1.0)
    first_re = jnp.dot(cos_block, gathered, precision=three_pass, preferred_element_type=jnp.float32)
    first_im = jnp.dot(sin_block, gathered, precision=three_pass, preferred_element_type=jnp.float32)
    global_pos = flat_index * parts + jnp.arange(parts, dtype=jnp.int32)
    twist_cos, twist_sin = turns(block_index[:, None] * global_pos[None, :], total_rows, -1.0)
    first_re, first_im = complex_mul(first_re, first_im, twist_cos, twist_sin)
    ordered = (
        jnp.stack([first_re, first_im])
        .reshape(2, n_cols, n_rows, parts)
        .transpose(0, 2, 1, 3)
        .reshape(2, devices * parts)
    )
    columns = regroup(ordered)
    coef_re, coef_im = local_dft(columns[0], columns[1], -1.0)
    coef_re = coef_re / total_rows
    coef_im = coef_im / total_rows
    seg_dev = SEGMENTS // n_cols
    seg_rows = rows_dev // SEGMENTS
    packed = jnp.stack([coef_re, coef_im]).reshape(2, n_cols, seg_dev, seg_rows)
    owned = column_relay(packed)
    owned = owned.transpose(0, 2, 3, 1).reshape(2, seg_dev, seg_rows * n_cols)
    short = seg_rows * n_cols
    band = short * SEGMENTS
    phase_index = jnp.arange(SEGMENTS, dtype=jnp.int32)
    short_index = jnp.arange(short, dtype=jnp.int32)
    phase_cos, phase_sin = turns(phase_index[:, None] * short_index[None, :], band, 1.0)
    spread_re, spread_im = complex_mul(
        owned[0][:, None, :], owned[1][:, None, :], phase_cos, phase_sin
    )
    lift_re, lift_im = lift_dft(spread_re, spread_im, 1.0)
    band_index = jnp.arange(band, dtype=jnp.int32)
    shift_cos, shift_sin = turns(band_index * row_index, total_rows, 1.0)
    lift_re, lift_im = complex_mul(lift_re, lift_im, shift_cos, shift_sin)
    small = band // devices
    lifted = (
        jnp.stack([lift_re, lift_im])
        .reshape(2, seg_dev, devices, small)
        .transpose(0, 2, 1, 3)
    )
    arrived = regroup(lifted).reshape(2, n_rows, n_cols, seg_dev, small)
    row_ids = jnp.arange(n_rows, dtype=jnp.int32)
    cos_rows, sin_rows = turns(row_ids[:, None] * row_ids[None, :], n_rows, 1.0)
    summed_re = jnp.einsum("ab,bcsu->csau", cos_rows, arrived[0], precision=three_pass) - jnp.einsum(
        "ab,bcsu->csau", sin_rows, arrived[1], precision=three_pass
    )
    summed_im = jnp.einsum("ab,bcsu->csau", sin_rows, arrived[0], precision=three_pass) + jnp.einsum(
        "ab,bcsu->csau", cos_rows, arrived[1], precision=three_pass
    )
    values = jnp.stack([summed_re, summed_im]).reshape(2, SEGMENTS, n_rows, small)
    leaf_count = n_rows * small
    real_part = values[0].reshape(SEGMENTS, leaf_count)
    imag_part = values[1].reshape(SEGMENTS, leaf_count)
    zeros = jnp.zeros((DIGEST, leaf_count), jnp.float32)
    state = permute(jnp.concatenate([zeros, real_part], axis=0), hash_mds, hash_rc)
    state = state + jnp.concatenate([zeros, imag_part], axis=0)
    state = permute(state, hash_mds, hash_rc)
    return state[:DIGEST].reshape(DIGEST, n_rows, small)


def solution(mesh):
    in_specs = (
        P(None, ("rows", "cols")),
        P(None, ("rows", "cols")),
        P(),
        P(),
        P(),
        P(),
        P(("rows", "cols")),
        P(),
        P(),
    )
    out_specs = P(None, None, ("rows", "cols"))
    return jax.shard_map(
        on_device, mesh=mesh, in_specs=in_specs, out_specs=out_specs, check_vma=False
    )
```

```python
import math

import jax
import jax.numpy as jnp
from jax import lax
from jax.sharding import PartitionSpec as P

BLOWUP = 8
SEGMENTS = 8
DIGEST = 4
ROUNDS = 2


highest = lax.Precision.HIGHEST
three_pass = lax.Precision.HIGH


def from_behind(array, axis, by):
    count = lax.axis_size(axis)
    return lax.ppermute(array, axis, [(i, (i + by) % count) for i in range(count)])


def entering(value, axis):
    count, mine = (lax.axis_size(axis), lax.axis_index(axis))
    spread = jnp.broadcast_to(value, (count,))
    pieces = lax.all_to_all(spread, axis, 0, 0, tiled=True)
    earlier = jnp.arange(count, dtype=jnp.int32) < mine
    return jnp.sum(jnp.where(earlier, pieces, jnp.zeros_like(pieces)))


def squash(value):
    return value * lax.rsqrt(1.0 + value * value)


def permute(state, hash_mds, hash_rc):
    for step in range(ROUNDS):
        state = (
            jnp.dot(hash_mds, squash(state), precision=highest, preferred_element_type=jnp.float32)
            + hash_rc[step][:, None]
        )
    return state


def turns(product, modulus, sign):
    angle = sign * 2.0 * math.pi / modulus * (product % modulus).astype(jnp.float32)
    return (jnp.cos(angle), jnp.sin(angle))


def complex_mul(left_re, left_im, right_re, right_im):
    return (left_re * right_re - left_im * right_im, left_re * right_im + left_im * right_re)


def block_table(cos_t, sin_t):
    return jnp.concatenate(
        [jnp.concatenate([cos_t, -sin_t], axis=1), jnp.concatenate([sin_t, cos_t], axis=1)], axis=0
    )


def local_dft(values_re, values_im, sign):
    length = values_re.shape[-1]
    first = 128
    second = length // first
    leading = values_re.shape[:-1]
    stacked = jnp.concatenate(
        [values_re.reshape(leading + (first, second)), values_im.reshape(leading + (first, second))],
        axis=-2,
    )
    index_one = jnp.arange(first, dtype=jnp.int32)
    index_two = jnp.arange(second, dtype=jnp.int32)
    table_one = block_table(*turns(index_one[:, None] * index_one[None, :], first, sign))
    section = jnp.einsum("kn,...nm->...km", table_one, stacked, precision=three_pass)
    section_re, section_im = section[..., :first, :], section[..., first:, :]
    twist_cos, twist_sin = turns(index_one[:, None] * index_two[None, :], length, sign)
    section_re, section_im = complex_mul(section_re, section_im, twist_cos, twist_sin)
    table_two = block_table(*turns(index_two[:, None] * index_two[None, :], second, sign))
    both = jnp.concatenate([section_re, section_im], axis=-1)
    final = jnp.einsum("jn,...kn->...jk", table_two, both, precision=three_pass)
    final_re = final[..., :second, :].reshape(leading + (length,))
    final_im = final[..., second:, :].reshape(leading + (length,))
    return (final_re, final_im)


def lift_dft(values_re, values_im, sign):
    segs, phases, length = values_re.shape
    first = 128
    second = length // first
    stacked = jnp.concatenate(
        [values_re.reshape(segs, phases, first, second), values_im.reshape(segs, phases, first, second)],
        axis=2,
    )
    index_one = jnp.arange(first, dtype=jnp.int32)
    index_two = jnp.arange(second, dtype=jnp.int32)
    table_one = block_table(*turns(index_one[:, None] * index_one[None, :], first, sign))
    section = jnp.einsum("kn,spnm->skpm", table_one, stacked, precision=three_pass)
    section_re, section_im = section[:, :first], section[:, first:]
    twist_cos, twist_sin = turns(index_one[:, None] * index_two[None, :], length, sign)
    section_re, section_im = complex_mul(
        section_re, section_im, twist_cos[:, None, :], twist_sin[:, None, :]
    )
    both = jnp.concatenate([section_re, section_im], axis=-1).reshape(segs, first * phases, 2 * second)
    table_two = block_table(*turns(index_two[:, None] * index_two[None, :], second, sign))
    final = jnp.einsum("jm,sxm->sjx", table_two, both, precision=three_pass)
    final_re = final[:, :second].reshape(segs, length * phases)
    final_im = final[:, second:].reshape(segs, length * phases)
    return (final_re, final_im)


def regroup(values):
    return lax.all_to_all(values, ("rows", "cols"), split_axis=1, concat_axis=1, tiled=True)


def column_relay(values):
    return lax.all_to_all(values, "cols", split_axis=1, concat_axis=1, tiled=True)


def on_device(trace, selectors, mds, quad, alpha, challenges, divisor_inv, hash_mds, hash_rc):
    width = trace.shape[0]
    rows_dev = trace.shape[1]
    n_rows = lax.axis_size("rows")
    n_cols = lax.axis_size("cols")
    devices = n_rows * n_cols
    total_rows = rows_dev * devices
    flat_index = lax.axis_index(("rows", "cols"))
    row_index = lax.axis_index("rows")
    rim = from_behind(trace[:, :BLOWUP], ("rows", "cols"), -1)
    extended = jnp.concatenate([trace, rim], axis=1)
    following = extended[:, BLOWUP:]
    linear = jnp.dot(mds, trace, precision=highest, preferred_element_type=jnp.float32)
    cons = following - linear - quad[:, None] * trace * trace
    step_size = challenges[0] / jnp.sqrt(jnp.float32(total_rows))
    gamma = challenges[1]
    numer = 1.0 + step_size * (extended[0] + gamma * extended[1])
    denom = 1.0 + step_size * (extended[2] + gamma * extended[3])
    ratio_log = jnp.log(numer) - jnp.log(denom)
    own_terms = ratio_log[:rows_dev]
    running_sum = jnp.cumsum(own_terms)
    offset = entering(running_sum[-1], ("rows", "cols"))
    running = jnp.exp(offset + running_sum - own_terms)
    window = own_terms
    for shift_step in range(1, BLOWUP):
        window = window + ratio_log[shift_step : shift_step + rows_dev]
    grand = running * (jnp.exp(window) * denom[:rows_dev] - numer[:rows_dev]) / step_size
    picked = selectors.astype(jnp.float32)
    combined = (
        jnp.sum(alpha[:width, None] * picked[:width] * cons, axis=0)
        + alpha[width] * picked[width] * grand
    )
    quotient = divisor_inv * combined
    parts = rows_dev // devices
    gathered = regroup(quotient.reshape(1, rows_dev)).reshape(devices, parts)
    block_index = jnp.arange(devices, dtype=jnp.int32)
    cos_block, sin_block = turns(block_index[:, None] * block_index[None, :], devices, -1.0)
    first_re = jnp.dot(cos_block, gathered, precision=three_pass, preferred_element_type=jnp.float32)
    first_im = jnp.dot(sin_block, gathered, precision=three_pass, preferred_element_type=jnp.float32)
    global_pos = flat_index * parts + jnp.arange(parts, dtype=jnp.int32)
    twist_cos, twist_sin = turns(block_index[:, None] * global_pos[None, :], total_rows, -1.0)
    first_re, first_im = complex_mul(first_re, first_im, twist_cos, twist_sin)
    ordered = (
        jnp.stack([first_re, first_im])
        .reshape(2, n_cols, n_rows, parts)
        .transpose(0, 2, 1, 3)
        .reshape(2, devices * parts)
    )
    columns = regroup(ordered)
    coef_re, coef_im = local_dft(columns[0], columns[1], -1.0)
    coef_re = coef_re / total_rows
    coef_im = coef_im / total_rows
    seg_dev = SEGMENTS // n_cols
    seg_rows = rows_dev // SEGMENTS
    packed = jnp.stack([coef_re, coef_im]).reshape(2, n_cols, seg_dev, seg_rows)
    owned = column_relay(packed)
    owned = owned.transpose(0, 2, 3, 1).reshape(2, seg_dev, seg_rows * n_cols)
    short = seg_rows * n_cols
    band = short * SEGMENTS
    phase_index = jnp.arange(SEGMENTS, dtype=jnp.int32)
    short_index = jnp.arange(short, dtype=jnp.int32)
    phase_cos, phase_sin = turns(phase_index[:, None] * short_index[None, :], band, 1.0)
    spread_re, spread_im = complex_mul(
        owned[0][:, None, :], owned[1][:, None, :], phase_cos, phase_sin
    )
    lift_re, lift_im = lift_dft(spread_re, spread_im, 1.0)
    band_index = jnp.arange(band, dtype=jnp.int32)
    shift_cos, shift_sin = turns(band_index * row_index, total_rows, 1.0)
    lift_re, lift_im = complex_mul(lift_re, lift_im, shift_cos, shift_sin)
    small = band // devices
    lifted = (
        jnp.stack([lift_re, lift_im])
        .reshape(2, seg_dev, devices, small)
        .transpose(0, 2, 1, 3)
    )
    arrived = regroup(lifted).reshape(2, n_rows, n_cols, seg_dev, small)
    row_ids = jnp.arange(n_rows, dtype=jnp.int32)
    cos_rows, sin_rows = turns(row_ids[:, None] * row_ids[None, :], n_rows, 1.0)
    summed_re = jnp.einsum("ab,bcsu->csau", cos_rows, arrived[0], precision=three_pass) - jnp.einsum(
        "ab,bcsu->csau", sin_rows, arrived[1], precision=three_pass
    )
    summed_im = jnp.einsum("ab,bcsu->csau", sin_rows, arrived[0], precision=three_pass) + jnp.einsum(
        "ab,bcsu->csau", cos_rows, arrived[1], precision=three_pass
    )
    values = jnp.stack([summed_re, summed_im]).reshape(2, SEGMENTS, n_rows, small)
    leaf_count = n_rows * small
    real_part = values[0].reshape(SEGMENTS, leaf_count)
    imag_part = values[1].reshape(SEGMENTS, leaf_count)
    zeros = jnp.zeros((DIGEST, leaf_count), jnp.float32)
    state = permute(jnp.concatenate([zeros, real_part], axis=0), hash_mds, hash_rc)
    state = state + jnp.concatenate([zeros, imag_part], axis=0)
    state = permute(state, hash_mds, hash_rc)
    return state[:DIGEST].reshape(DIGEST, n_rows, small)


def solution(mesh):
    in_specs = (
        P(None, ("rows", "cols")),
        P(None, ("rows", "cols")),
        P(),
        P(),
        P(),
        P(),
        P(("rows", "cols")),
        P(),
        P(),
    )
    out_specs = P(None, None, ("rows", "cols"))
    return jax.shard_map(
        on_device, mesh=mesh, in_specs=in_specs, out_specs=out_specs, check_vma=False
    )
```

```python
import math

import jax
import jax.numpy as jnp
from jax import lax
from jax.sharding import PartitionSpec as P

BLOWUP = 8
SEGMENTS = 8
DIGEST = 4
ROUNDS = 2


highest = lax.Precision.HIGHEST
three_pass = lax.Precision.HIGH


def from_behind(array, axis, by):
    count = lax.axis_size(axis)
    return lax.ppermute(array, axis, [(i, (i + by) % count) for i in range(count)])


def entering(value, axis):
    count, mine = (lax.axis_size(axis), lax.axis_index(axis))
    spread = jnp.broadcast_to(value, (count,))
    pieces = lax.all_to_all(spread, axis, 0, 0, tiled=True)
    earlier = jnp.arange(count, dtype=jnp.int32) < mine
    return jnp.sum(jnp.where(earlier, pieces, jnp.zeros_like(pieces)))


def squash(value):
    return value * lax.rsqrt(1.0 + value * value)


def permute(state, hash_mds, hash_rc):
    for step in range(ROUNDS):
        state = (
            jnp.dot(hash_mds, squash(state), precision=highest, preferred_element_type=jnp.float32)
            + hash_rc[step][:, None]
        )
    return state


def turns(product, modulus, sign):
    angle = sign * 2.0 * math.pi / modulus * (product % modulus).astype(jnp.float32)
    return (jnp.cos(angle), jnp.sin(angle))


def complex_mul(left_re, left_im, right_re, right_im):
    return (left_re * right_re - left_im * right_im, left_re * right_im + left_im * right_re)


def block_table(cos_t, sin_t):
    return jnp.concatenate(
        [jnp.concatenate([cos_t, -sin_t], axis=1), jnp.concatenate([sin_t, cos_t], axis=1)], axis=0
    )


def local_dft(values_re, values_im, sign):
    length = values_re.shape[-1]
    first = 128
    second = length // first
    leading = values_re.shape[:-1]
    stacked = jnp.concatenate(
        [values_re.reshape(leading + (first, second)), values_im.reshape(leading + (first, second))],
        axis=-2,
    )
    index_one = jnp.arange(first, dtype=jnp.int32)
    index_two = jnp.arange(second, dtype=jnp.int32)
    table_one = block_table(*turns(index_one[:, None] * index_one[None, :], first, sign))
    section = jnp.einsum("kn,...nm->...km", table_one, stacked, precision=three_pass)
    section_re, section_im = section[..., :first, :], section[..., first:, :]
    twist_cos, twist_sin = turns(index_one[:, None] * index_two[None, :], length, sign)
    section_re, section_im = complex_mul(section_re, section_im, twist_cos, twist_sin)
    table_two = block_table(*turns(index_two[:, None] * index_two[None, :], second, sign))
    both = jnp.concatenate([section_re, section_im], axis=-1)
    final = jnp.einsum("jn,...kn->...jk", table_two, both, precision=three_pass)
    final_re = final[..., :second, :].reshape(leading + (length,))
    final_im = final[..., second:, :].reshape(leading + (length,))
    return (final_re, final_im)


def lift_dft(values_re, values_im, sign):
    segs, phases, length = values_re.shape
    first = 128
    second = length // first
    stacked = jnp.concatenate(
        [values_re.reshape(segs, phases, first, second), values_im.reshape(segs, phases, first, second)],
        axis=2,
    )
    index_one = jnp.arange(first, dtype=jnp.int32)
    index_two = jnp.arange(second, dtype=jnp.int32)
    table_one = block_table(*turns(index_one[:, None] * index_one[None, :], first, sign))
    section = jnp.einsum("kn,spnm->skpm", table_one, stacked, precision=three_pass)
    section_re, section_im = section[:, :first], section[:, first:]
    twist_cos, twist_sin = turns(index_one[:, None] * index_two[None, :], length, sign)
    section_re, section_im = complex_mul(
        section_re, section_im, twist_cos[:, None, :], twist_sin[:, None, :]
    )
    both = jnp.concatenate([section_re, section_im], axis=-1).reshape(segs, first * phases, 2 * second)
    table_two = block_table(*turns(index_two[:, None] * index_two[None, :], second, sign))
    final = jnp.einsum("jm,sxm->sjx", table_two, both, precision=three_pass)
    final_re = final[:, :second].reshape(segs, length * phases)
    final_im = final[:, second:].reshape(segs, length * phases)
    return (final_re, final_im)


def lift_eval(coef_re, coef_im, phases, row_index, total_rows, devices):
    segs, length = coef_re.shape
    first = 128
    second = length // first
    band = length * phases
    stacked = jnp.concatenate(
        [coef_re.reshape(segs, first, second), coef_im.reshape(segs, first, second)], axis=1
    )
    index_one = jnp.arange(first, dtype=jnp.int32)
    index_two = jnp.arange(second, dtype=jnp.int32)
    index_p = jnp.arange(phases, dtype=jnp.int32)
    k_one = index_one[None, :, None]
    n_one = index_one[None, None, :]
    p_one = index_p[:, None, None]
    angle_one = (
        (k_one * n_one % first) * (total_rows // first)
        + (p_one * n_one) * (total_rows // (first * phases))
        + (phases * k_one + p_one) * row_index
    )
    cos_one, sin_one = turns(angle_one, total_rows, 1.0)
    table_one = jnp.concatenate(
        [jnp.concatenate([cos_one, -sin_one], axis=2), jnp.concatenate([sin_one, cos_one], axis=2)],
        axis=1,
    )
    section = jnp.einsum("pkn,snm->skpm", table_one, stacked, precision=three_pass)
    section_re, section_im = section[:, :first], section[:, first:]
    twist = (phases * index_one[:, None, None] + index_p[None, :, None]) * index_two[None, None, :]
    twist_cos, twist_sin = turns(twist, band, 1.0)
    section_re, section_im = complex_mul(section_re, section_im, twist_cos, twist_sin)
    both = jnp.concatenate([section_re, section_im], axis=-1).reshape(segs, first * phases, 2 * second)
    angle_two = (index_two[:, None] * index_two[None, :] % second) * (total_rows // second) + (
        index_two[:, None] * row_index * (first * phases)
    )
    table_two = block_table(*turns(angle_two, total_rows, 1.0))
    final = jnp.einsum("jm,sxm->sjx", table_two, both, precision=three_pass)
    return final.reshape(segs, 2, devices, band // devices).transpose(1, 2, 0, 3)


def regroup(values):
    return lax.all_to_all(values, ("rows", "cols"), split_axis=1, concat_axis=1, tiled=True)


def column_relay(values):
    return lax.all_to_all(values, "cols", split_axis=1, concat_axis=1, tiled=True)


def on_device(trace, selectors, mds, quad, alpha, challenges, divisor_inv, hash_mds, hash_rc):
    width = trace.shape[0]
    rows_dev = trace.shape[1]
    n_rows = lax.axis_size("rows")
    n_cols = lax.axis_size("cols")
    devices = n_rows * n_cols
    total_rows = rows_dev * devices
    flat_index = lax.axis_index(("rows", "cols"))
    row_index = lax.axis_index("rows")
    rim = from_behind(trace[:, :BLOWUP], ("rows", "cols"), -1)
    extended = jnp.concatenate([trace, rim], axis=1)
    following = extended[:, BLOWUP:]
    linear = jnp.dot(mds, trace, precision=highest, preferred_element_type=jnp.float32)
    cons = following - linear - quad[:, None] * trace * trace
    step_size = challenges[0] / jnp.sqrt(jnp.float32(total_rows))
    gamma = challenges[1]
    numer = 1.0 + step_size * (extended[0] + gamma * extended[1])
    denom = 1.0 + step_size * (extended[2] + gamma * extended[3])
    ratio_log = jnp.log(numer) - jnp.log(denom)
    own_terms = ratio_log[:rows_dev]
    running_sum = jnp.cumsum(own_terms)
    offset = entering(running_sum[-1], ("rows", "cols"))
    running = jnp.exp(offset + running_sum - own_terms)
    window = own_terms
    for shift_step in range(1, BLOWUP):
        window = window + ratio_log[shift_step : shift_step + rows_dev]
    grand = running * (jnp.exp(window) * denom[:rows_dev] - numer[:rows_dev]) / step_size
    picked = selectors.astype(jnp.float32)
    combined = (
        jnp.sum(alpha[:width, None] * picked[:width] * cons, axis=0)
        + alpha[width] * picked[width] * grand
    )
    quotient = divisor_inv * combined
    parts = rows_dev // devices
    gathered = regroup(quotient.reshape(1, rows_dev)).reshape(devices, parts)
    block_index = jnp.arange(devices, dtype=jnp.int32)
    cos_block, sin_block = turns(block_index[:, None] * block_index[None, :], devices, -1.0)
    first_re = jnp.dot(cos_block, gathered, precision=three_pass, preferred_element_type=jnp.float32)
    first_im = jnp.dot(sin_block, gathered, precision=three_pass, preferred_element_type=jnp.float32)
    global_pos = flat_index * parts + jnp.arange(parts, dtype=jnp.int32)
    twist_cos, twist_sin = turns(block_index[:, None] * global_pos[None, :], total_rows, -1.0)
    first_re, first_im = complex_mul(first_re, first_im, twist_cos, twist_sin)
    ordered = (
        jnp.stack([first_re, first_im])
        .reshape(2, n_cols, n_rows, parts)
        .transpose(0, 2, 1, 3)
        .reshape(2, devices * parts)
    )
    columns = regroup(ordered)
    coef_re, coef_im = local_dft(columns[0], columns[1], -1.0)
    coef_re = coef_re / total_rows
    coef_im = coef_im / total_rows
    seg_dev = SEGMENTS // n_cols
    seg_rows = rows_dev // SEGMENTS
    packed = jnp.stack([coef_re, coef_im]).reshape(2, n_cols, seg_dev, seg_rows)
    owned = column_relay(packed)
    owned = owned.transpose(0, 2, 3, 1).reshape(2, seg_dev, seg_rows * n_cols)
    short = seg_rows * n_cols
    band = short * SEGMENTS
    small = band // devices
    lifted = lift_eval(owned[0], owned[1], SEGMENTS, row_index, total_rows, devices)
    arrived = regroup(lifted).reshape(2, n_rows, n_cols, seg_dev, small)
    row_ids = jnp.arange(n_rows, dtype=jnp.int32)
    cos_rows, sin_rows = turns(row_ids[:, None] * row_ids[None, :], n_rows, 1.0)
    summed_re = jnp.einsum("ab,bcsu->csau", cos_rows, arrived[0], precision=three_pass) - jnp.einsum(
        "ab,bcsu->csau", sin_rows, arrived[1], precision=three_pass
    )
    summed_im = jnp.einsum("ab,bcsu->csau", sin_rows, arrived[0], precision=three_pass) + jnp.einsum(
        "ab,bcsu->csau", cos_rows, arrived[1], precision=three_pass
    )
    values = jnp.stack([summed_re, summed_im]).reshape(2, SEGMENTS, n_rows, small)
    leaf_count = n_rows * small
    real_part = values[0].reshape(SEGMENTS, leaf_count)
    imag_part = values[1].reshape(SEGMENTS, leaf_count)
    zeros = jnp.zeros((DIGEST, leaf_count), jnp.float32)
    state = permute(jnp.concatenate([zeros, real_part], axis=0), hash_mds, hash_rc)
    state = state + jnp.concatenate([zeros, imag_part], axis=0)
    state = permute(state, hash_mds, hash_rc)
    return state[:DIGEST].reshape(DIGEST, n_rows, small)


def solution(mesh):
    in_specs = (
        P(None, ("rows", "cols")),
        P(None, ("rows", "cols")),
        P(),
        P(),
        P(),
        P(),
        P(("rows", "cols")),
        P(),
        P(),
    )
    out_specs = P(None, None, ("rows", "cols"))
    return jax.shard_map(
        on_device, mesh=mesh, in_specs=in_specs, out_specs=out_specs, check_vma=False
    )
```

```python
import math

import jax
import jax.numpy as jnp
from jax import lax
from jax.sharding import PartitionSpec as P

BLOWUP = 8
SEGMENTS = 8
DIGEST = 4
ROUNDS = 2


highest = lax.Precision.HIGHEST
three_pass = lax.Precision.HIGH


def from_behind(array, axis, by):
    count = lax.axis_size(axis)
    return lax.ppermute(array, axis, [(i, (i + by) % count) for i in range(count)])


def entering(value, axis):
    count, mine = (lax.axis_size(axis), lax.axis_index(axis))
    spread = jnp.broadcast_to(value, (count,))
    pieces = lax.all_to_all(spread, axis, 0, 0, tiled=True)
    earlier = jnp.arange(count, dtype=jnp.int32) < mine
    return jnp.sum(jnp.where(earlier, pieces, jnp.zeros_like(pieces)))


def squash(value):
    return value * lax.rsqrt(1.0 + value * value)


def permute(state, hash_mds, hash_rc):
    for step in range(ROUNDS):
        state = (
            jnp.dot(hash_mds, squash(state), precision=highest, preferred_element_type=jnp.float32)
            + hash_rc[step][:, None]
        )
    return state


def turns(product, modulus, sign):
    angle = sign * 2.0 * math.pi / modulus * (product % modulus).astype(jnp.float32)
    return (jnp.cos(angle), jnp.sin(angle))


def complex_mul(left_re, left_im, right_re, right_im):
    return (left_re * right_re - left_im * right_im, left_re * right_im + left_im * right_re)


def block_table(cos_t, sin_t):
    return jnp.concatenate(
        [jnp.concatenate([cos_t, -sin_t], axis=1), jnp.concatenate([sin_t, cos_t], axis=1)], axis=0
    )


def local_dft(values_re, values_im, sign):
    length = values_re.shape[-1]
    first = 128
    second = length // first
    leading = values_re.shape[:-1]
    stacked = jnp.concatenate(
        [values_re.reshape(leading + (first, second)), values_im.reshape(leading + (first, second))],
        axis=-2,
    )
    index_one = jnp.arange(first, dtype=jnp.int32)
    index_two = jnp.arange(second, dtype=jnp.int32)
    table_one = block_table(*turns(index_one[:, None] * index_one[None, :], first, sign))
    section = jnp.einsum("kn,...nm->...km", table_one, stacked, precision=three_pass)
    section_re, section_im = section[..., :first, :], section[..., first:, :]
    twist_cos, twist_sin = turns(index_one[:, None] * index_two[None, :], length, sign)
    section_re, section_im = complex_mul(section_re, section_im, twist_cos, twist_sin)
    table_two = block_table(*turns(index_two[:, None] * index_two[None, :], second, sign))
    both = jnp.concatenate([section_re, section_im], axis=-1)
    final = jnp.einsum("jn,...kn->...jk", table_two, both, precision=three_pass)
    final_re = final[..., :second, :].reshape(leading + (length,))
    final_im = final[..., second:, :].reshape(leading + (length,))
    return (final_re, final_im)


def lift_dft(values_re, values_im, sign):
    segs, phases, length = values_re.shape
    first = 128
    second = length // first
    stacked = jnp.concatenate(
        [values_re.reshape(segs, phases, first, second), values_im.reshape(segs, phases, first, second)],
        axis=2,
    )
    index_one = jnp.arange(first, dtype=jnp.int32)
    index_two = jnp.arange(second, dtype=jnp.int32)
    table_one = block_table(*turns(index_one[:, None] * index_one[None, :], first, sign))
    section = jnp.einsum("kn,spnm->skpm", table_one, stacked, precision=three_pass)
    section_re, section_im = section[:, :first], section[:, first:]
    twist_cos, twist_sin = turns(index_one[:, None] * index_two[None, :], length, sign)
    section_re, section_im = complex_mul(
        section_re, section_im, twist_cos[:, None, :], twist_sin[:, None, :]
    )
    both = jnp.concatenate([section_re, section_im], axis=-1).reshape(segs, first * phases, 2 * second)
    table_two = block_table(*turns(index_two[:, None] * index_two[None, :], second, sign))
    final = jnp.einsum("jm,sxm->sjx", table_two, both, precision=three_pass)
    final_re = final[:, :second].reshape(segs, length * phases)
    final_im = final[:, second:].reshape(segs, length * phases)
    return (final_re, final_im)


def lift_eval(coef_re, coef_im, phases, row_index, total_rows, devices):
    segs, length = coef_re.shape
    first = 128
    second = length // first
    band = length * phases
    stacked = jnp.concatenate(
        [coef_re.reshape(segs, first, second), coef_im.reshape(segs, first, second)], axis=1
    )
    index_one = jnp.arange(first, dtype=jnp.int32)
    index_two = jnp.arange(second, dtype=jnp.int32)
    index_p = jnp.arange(phases, dtype=jnp.int32)
    k_one = index_one[None, :, None]
    n_one = index_one[None, None, :]
    p_one = index_p[:, None, None]
    angle_one = (
        (k_one * n_one % first) * (total_rows // first)
        + (p_one * n_one) * (total_rows // (first * phases))
        + (phases * k_one + p_one) * row_index
    )
    cos_one, sin_one = turns(angle_one, total_rows, 1.0)
    table_one = jnp.concatenate(
        [jnp.concatenate([cos_one, -sin_one], axis=2), jnp.concatenate([sin_one, cos_one], axis=2)],
        axis=1,
    )
    section = jnp.einsum("pkn,snm->skpm", table_one, stacked, precision=three_pass)
    section_re, section_im = section[:, :first], section[:, first:]
    twist = (phases * index_one[:, None, None] + index_p[None, :, None]) * index_two[None, None, :]
    twist_cos, twist_sin = turns(twist, band, 1.0)
    section_re, section_im = complex_mul(section_re, section_im, twist_cos, twist_sin)
    both = jnp.concatenate([section_re, section_im], axis=-1).reshape(segs, first * phases, 2 * second)
    angle_two = (index_two[:, None] * index_two[None, :] % second) * (total_rows // second) + (
        index_two[:, None] * row_index * (first * phases)
    )
    cos_two, sin_two = turns(angle_two, total_rows, 1.0)
    table_two = jnp.stack(
        [jnp.concatenate([cos_two, -sin_two], axis=1), jnp.concatenate([sin_two, cos_two], axis=1)],
        axis=1,
    ).reshape(2 * second, 2 * second)
    final = jnp.einsum("jm,sxm->sjx", table_two, both, precision=three_pass)
    rows_per = 2 * second // devices
    return final.reshape(segs, devices, rows_per, first * phases).transpose(1, 0, 2, 3)


def regroup(values):
    return lax.all_to_all(values, ("rows", "cols"), split_axis=1, concat_axis=1, tiled=True)


def column_relay(values):
    return lax.all_to_all(values, "cols", split_axis=1, concat_axis=1, tiled=True)


def on_device(trace, selectors, mds, quad, alpha, challenges, divisor_inv, hash_mds, hash_rc):
    width = trace.shape[0]
    rows_dev = trace.shape[1]
    n_rows = lax.axis_size("rows")
    n_cols = lax.axis_size("cols")
    devices = n_rows * n_cols
    total_rows = rows_dev * devices
    flat_index = lax.axis_index(("rows", "cols"))
    row_index = lax.axis_index("rows")
    rim = from_behind(trace[:, :BLOWUP], ("rows", "cols"), -1)
    extended = jnp.concatenate([trace, rim], axis=1)
    following = extended[:, BLOWUP:]
    linear = jnp.dot(mds, trace, precision=highest, preferred_element_type=jnp.float32)
    cons = following - linear - quad[:, None] * trace * trace
    step_size = challenges[0] / jnp.sqrt(jnp.float32(total_rows))
    gamma = challenges[1]
    numer = 1.0 + step_size * (extended[0] + gamma * extended[1])
    denom = 1.0 + step_size * (extended[2] + gamma * extended[3])
    ratio_log = jnp.log(numer) - jnp.log(denom)
    own_terms = ratio_log[:rows_dev]
    running_sum = jnp.cumsum(own_terms)
    offset = entering(running_sum[-1], ("rows", "cols"))
    running = jnp.exp(offset + running_sum - own_terms)
    window = own_terms
    for shift_step in range(1, BLOWUP):
        window = window + ratio_log[shift_step : shift_step + rows_dev]
    grand = running * (jnp.exp(window) * denom[:rows_dev] - numer[:rows_dev]) / step_size
    picked = selectors.astype(jnp.float32)
    combined = (
        jnp.sum(alpha[:width, None] * picked[:width] * cons, axis=0)
        + alpha[width] * picked[width] * grand
    )
    quotient = divisor_inv * combined
    parts = rows_dev // devices
    gathered = regroup(quotient.reshape(1, rows_dev)).reshape(devices, parts)
    block_index = jnp.arange(devices, dtype=jnp.int32)
    cos_block, sin_block = turns(block_index[:, None] * block_index[None, :], devices, -1.0)
    first_re = jnp.dot(cos_block, gathered, precision=three_pass, preferred_element_type=jnp.float32)
    first_im = jnp.dot(sin_block, gathered, precision=three_pass, preferred_element_type=jnp.float32)
    global_pos = flat_index * parts + jnp.arange(parts, dtype=jnp.int32)
    twist_cos, twist_sin = turns(block_index[:, None] * global_pos[None, :], total_rows, -1.0)
    first_re, first_im = complex_mul(first_re, first_im, twist_cos, twist_sin)
    ordered = (
        jnp.stack([first_re, first_im])
        .reshape(2, n_cols, n_rows, parts)
        .transpose(0, 2, 1, 3)
        .reshape(2, devices * parts)
    )
    columns = regroup(ordered)
    coef_re, coef_im = local_dft(columns[0], columns[1], -1.0)
    coef_re = coef_re / total_rows
    coef_im = coef_im / total_rows
    seg_dev = SEGMENTS // n_cols
    seg_rows = rows_dev // SEGMENTS
    packed = jnp.stack([coef_re, coef_im]).reshape(2, n_cols, seg_dev, seg_rows)
    owned = column_relay(packed)
    owned = owned.transpose(0, 2, 3, 1).reshape(2, seg_dev, seg_rows * n_cols)
    short = seg_rows * n_cols
    band = short * SEGMENTS
    small = band // devices
    lifted = lift_eval(owned[0], owned[1], SEGMENTS, row_index, total_rows, devices)
    arrived = lax.all_to_all(lifted, ("rows", "cols"), 0, 0, tiled=True)
    arrived = arrived.reshape(n_rows, n_cols, seg_dev, -1, 2, lifted.shape[-1])
    arrived_re, arrived_im = arrived[:, :, :, :, 0], arrived[:, :, :, :, 1]
    row_ids = jnp.arange(n_rows, dtype=jnp.int32)
    cos_rows, sin_rows = turns(row_ids[:, None] * row_ids[None, :], n_rows, 1.0)
    summed_re = jnp.einsum("ab,bcsvu->csavu", cos_rows, arrived_re, precision=three_pass) - jnp.einsum(
        "ab,bcsvu->csavu", sin_rows, arrived_im, precision=three_pass
    )
    summed_im = jnp.einsum("ab,bcsvu->csavu", sin_rows, arrived_re, precision=three_pass) + jnp.einsum(
        "ab,bcsvu->csavu", cos_rows, arrived_im, precision=three_pass
    )
    values = jnp.stack([summed_re, summed_im]).reshape(2, SEGMENTS, n_rows, small)
    leaf_count = n_rows * small
    real_part = values[0].reshape(SEGMENTS, leaf_count)
    imag_part = values[1].reshape(SEGMENTS, leaf_count)
    zeros = jnp.zeros((DIGEST, leaf_count), jnp.float32)
    state = permute(jnp.concatenate([zeros, real_part], axis=0), hash_mds, hash_rc)
    state = state + jnp.concatenate([zeros, imag_part], axis=0)
    state = permute(state, hash_mds, hash_rc)
    return state[:DIGEST].reshape(DIGEST, n_rows, small)


def solution(mesh):
    in_specs = (
        P(None, ("rows", "cols")),
        P(None, ("rows", "cols")),
        P(),
        P(),
        P(),
        P(),
        P(("rows", "cols")),
        P(),
        P(),
    )
    out_specs = P(None, None, ("rows", "cols"))
    return jax.shard_map(
        on_device, mesh=mesh, in_specs=in_specs, out_specs=out_specs, check_vma=False
    )
```

```python
import math

import jax
import jax.numpy as jnp
from jax import lax
from jax.sharding import PartitionSpec as P

BLOWUP = 8
SEGMENTS = 8
DIGEST = 4
ROUNDS = 2


highest = lax.Precision.HIGHEST
three_pass = lax.Precision.HIGH


def from_behind(array, axis, by):
    count = lax.axis_size(axis)
    return lax.ppermute(array, axis, [(i, (i + by) % count) for i in range(count)])


def entering(value, axis):
    count, mine = (lax.axis_size(axis), lax.axis_index(axis))
    spread = jnp.broadcast_to(value, (count,))
    pieces = lax.all_to_all(spread, axis, 0, 0, tiled=True)
    earlier = jnp.arange(count, dtype=jnp.int32) < mine
    return jnp.sum(jnp.where(earlier, pieces, jnp.zeros_like(pieces)))


def squash(value):
    return value * lax.rsqrt(1.0 + value * value)


def permute(state, hash_mds, hash_rc):
    for step in range(ROUNDS):
        state = (
            jnp.dot(hash_mds, squash(state), precision=highest, preferred_element_type=jnp.float32)
            + hash_rc[step][:, None]
        )
    return state


def turns(product, modulus, sign):
    angle = sign * 2.0 * math.pi / modulus * (product % modulus).astype(jnp.float32)
    return (jnp.cos(angle), jnp.sin(angle))


def complex_mul(left_re, left_im, right_re, right_im):
    return (left_re * right_re - left_im * right_im, left_re * right_im + left_im * right_re)


def block_table(cos_t, sin_t):
    return jnp.concatenate(
        [jnp.concatenate([cos_t, -sin_t], axis=1), jnp.concatenate([sin_t, cos_t], axis=1)], axis=0
    )


def local_dft(values_re, values_im, sign):
    length = values_re.shape[-1]
    first = 128
    second = length // first
    leading = values_re.shape[:-1]
    stacked = jnp.concatenate(
        [values_re.reshape(leading + (first, second)), values_im.reshape(leading + (first, second))],
        axis=-2,
    )
    index_one = jnp.arange(first, dtype=jnp.int32)
    index_two = jnp.arange(second, dtype=jnp.int32)
    table_one = block_table(*turns(index_one[:, None] * index_one[None, :], first, sign))
    section = jnp.einsum("kn,...nm->...km", table_one, stacked, precision=three_pass)
    section_re, section_im = section[..., :first, :], section[..., first:, :]
    twist_cos, twist_sin = turns(index_one[:, None] * index_two[None, :], length, sign)
    section_re, section_im = complex_mul(section_re, section_im, twist_cos, twist_sin)
    table_two = block_table(*turns(index_two[:, None] * index_two[None, :], second, sign))
    both = jnp.concatenate([section_re, section_im], axis=-1)
    final = jnp.einsum("jn,...kn->...jk", table_two, both, precision=three_pass)
    final_re = final[..., :second, :].reshape(leading + (length,))
    final_im = final[..., second:, :].reshape(leading + (length,))
    return (final_re, final_im)


def lift_dft(values_re, values_im, sign):
    segs, phases, length = values_re.shape
    first = 128
    second = length // first
    stacked = jnp.concatenate(
        [values_re.reshape(segs, phases, first, second), values_im.reshape(segs, phases, first, second)],
        axis=2,
    )
    index_one = jnp.arange(first, dtype=jnp.int32)
    index_two = jnp.arange(second, dtype=jnp.int32)
    table_one = block_table(*turns(index_one[:, None] * index_one[None, :], first, sign))
    section = jnp.einsum("kn,spnm->skpm", table_one, stacked, precision=three_pass)
    section_re, section_im = section[:, :first], section[:, first:]
    twist_cos, twist_sin = turns(index_one[:, None] * index_two[None, :], length, sign)
    section_re, section_im = complex_mul(
        section_re, section_im, twist_cos[:, None, :], twist_sin[:, None, :]
    )
    both = jnp.concatenate([section_re, section_im], axis=-1).reshape(segs, first * phases, 2 * second)
    table_two = block_table(*turns(index_two[:, None] * index_two[None, :], second, sign))
    final = jnp.einsum("jm,sxm->sjx", table_two, both, precision=three_pass)
    final_re = final[:, :second].reshape(segs, length * phases)
    final_im = final[:, second:].reshape(segs, length * phases)
    return (final_re, final_im)


def regroup(values):
    return lax.all_to_all(values, ("rows", "cols"), split_axis=1, concat_axis=1, tiled=True)


def column_relay(values):
    return lax.all_to_all(values, "cols", split_axis=1, concat_axis=1, tiled=True)


def on_device(trace, selectors, mds, quad, alpha, challenges, divisor_inv, hash_mds, hash_rc):
    width = trace.shape[0]
    rows_dev = trace.shape[1]
    n_rows = lax.axis_size("rows")
    n_cols = lax.axis_size("cols")
    devices = n_rows * n_cols
    total_rows = rows_dev * devices
    flat_index = lax.axis_index(("rows", "cols"))
    row_index = lax.axis_index("rows")
    rim = from_behind(trace[:, :BLOWUP], ("rows", "cols"), -1)
    following = jnp.concatenate([trace[:, BLOWUP:], rim], axis=1)
    head = jnp.concatenate([trace[:4], rim[:4]], axis=1)
    linear = jnp.dot(mds, trace, precision=highest, preferred_element_type=jnp.float32)
    cons = following - linear - quad[:, None] * trace * trace
    step_size = challenges[0] / jnp.sqrt(jnp.float32(total_rows))
    gamma = challenges[1]
    numer = 1.0 + step_size * (head[0] + gamma * head[1])
    denom = 1.0 + step_size * (head[2] + gamma * head[3])
    ratio_log = jnp.log(numer) - jnp.log(denom)
    own_terms = ratio_log[:rows_dev]
    running_sum = jnp.cumsum(own_terms)
    offset = entering(running_sum[-1], ("rows", "cols"))
    running = jnp.exp(offset + running_sum - own_terms)
    window = own_terms
    for shift_step in range(1, BLOWUP):
        window = window + ratio_log[shift_step : shift_step + rows_dev]
    grand = running * (jnp.exp(window) * denom[:rows_dev] - numer[:rows_dev]) / step_size
    picked = selectors.astype(jnp.float32)
    combined = (
        jnp.sum(alpha[:width, None] * picked[:width] * cons, axis=0)
        + alpha[width] * picked[width] * grand
    )
    quotient = divisor_inv * combined
    parts = rows_dev // devices
    gathered = regroup(quotient.reshape(1, rows_dev)).reshape(devices, parts)
    block_index = jnp.arange(devices, dtype=jnp.int32)
    cos_block, sin_block = turns(block_index[:, None] * block_index[None, :], devices, -1.0)
    first_re = jnp.dot(cos_block, gathered, precision=three_pass, preferred_element_type=jnp.float32)
    first_im = jnp.dot(sin_block, gathered, precision=three_pass, preferred_element_type=jnp.float32)
    global_pos = flat_index * parts + jnp.arange(parts, dtype=jnp.int32)
    twist_cos, twist_sin = turns(block_index[:, None] * global_pos[None, :], total_rows, -1.0)
    first_re, first_im = complex_mul(first_re, first_im, twist_cos, twist_sin)
    ordered = (
        jnp.stack([first_re, first_im])
        .reshape(2, n_cols, n_rows, parts)
        .transpose(0, 2, 1, 3)
        .reshape(2, devices * parts)
    )
    columns = regroup(ordered)
    coef_re, coef_im = local_dft(columns[0], columns[1], -1.0)
    coef_re = coef_re / total_rows
    coef_im = coef_im / total_rows
    seg_dev = SEGMENTS // n_cols
    seg_rows = rows_dev // SEGMENTS
    packed = jnp.stack([coef_re, coef_im]).reshape(2, n_cols, seg_dev, seg_rows)
    owned = column_relay(packed)
    owned = owned.transpose(0, 2, 3, 1).reshape(2, seg_dev, seg_rows * n_cols)
    short = seg_rows * n_cols
    band = short * SEGMENTS
    phase_index = jnp.arange(SEGMENTS, dtype=jnp.int32)
    short_index = jnp.arange(short, dtype=jnp.int32)
    phase_cos, phase_sin = turns(phase_index[:, None] * short_index[None, :], band, 1.0)
    spread_re, spread_im = complex_mul(
        owned[0][:, None, :], owned[1][:, None, :], phase_cos, phase_sin
    )
    lift_re, lift_im = lift_dft(spread_re, spread_im, 1.0)
    band_index = jnp.arange(band, dtype=jnp.int32)
    shift_cos, shift_sin = turns(band_index * row_index, total_rows, 1.0)
    lift_re, lift_im = complex_mul(lift_re, lift_im, shift_cos, shift_sin)
    small = band // devices
    lifted = (
        jnp.stack([lift_re, lift_im])
        .reshape(2, seg_dev, devices, small)
        .transpose(0, 2, 1, 3)
    )
    arrived = regroup(lifted).reshape(2, n_rows, n_cols, seg_dev, small)
    row_ids = jnp.arange(n_rows, dtype=jnp.int32)
    cos_rows, sin_rows = turns(row_ids[:, None] * row_ids[None, :], n_rows, 1.0)
    summed_re = jnp.einsum("ab,bcsu->csau", cos_rows, arrived[0], precision=three_pass) - jnp.einsum(
        "ab,bcsu->csau", sin_rows, arrived[1], precision=three_pass
    )
    summed_im = jnp.einsum("ab,bcsu->csau", sin_rows, arrived[0], precision=three_pass) + jnp.einsum(
        "ab,bcsu->csau", cos_rows, arrived[1], precision=three_pass
    )
    values = jnp.stack([summed_re, summed_im]).reshape(2, SEGMENTS, n_rows, small)
    leaf_count = n_rows * small
    real_part = values[0].reshape(SEGMENTS, leaf_count)
    imag_part = values[1].reshape(SEGMENTS, leaf_count)
    zeros = jnp.zeros((DIGEST, leaf_count), jnp.float32)
    state = permute(jnp.concatenate([zeros, real_part], axis=0), hash_mds, hash_rc)
    state = state + jnp.concatenate([zeros, imag_part], axis=0)
    state = permute(state, hash_mds, hash_rc)
    return state[:DIGEST].reshape(DIGEST, n_rows, small)


def solution(mesh):
    in_specs = (
        P(None, ("rows", "cols")),
        P(None, ("rows", "cols")),
        P(),
        P(),
        P(),
        P(),
        P(("rows", "cols")),
        P(),
        P(),
    )
    out_specs = P(None, None, ("rows", "cols"))
    return jax.shard_map(
        on_device, mesh=mesh, in_specs=in_specs, out_specs=out_specs, check_vma=False
    )
```

```python
import math

import jax
import jax.numpy as jnp
from jax import lax
from jax.sharding import PartitionSpec as P

BLOWUP = 8
SEGMENTS = 8
DIGEST = 4
ROUNDS = 2


highest = lax.Precision.HIGHEST
three_pass = lax.Precision.HIGH


def from_behind(array, axis, by):
    count = lax.axis_size(axis)
    return lax.ppermute(array, axis, [(i, (i + by) % count) for i in range(count)])


def entering(value, axis):
    count, mine = (lax.axis_size(axis), lax.axis_index(axis))
    spread = jnp.broadcast_to(value, (count,))
    pieces = lax.all_to_all(spread, axis, 0, 0, tiled=True)
    earlier = jnp.arange(count, dtype=jnp.int32) < mine
    return jnp.sum(jnp.where(earlier, pieces, jnp.zeros_like(pieces)))


def squash(value):
    return value * lax.rsqrt(1.0 + value * value)


def permute(state, hash_mds, hash_rc):
    for step in range(ROUNDS):
        state = (
            jnp.dot(hash_mds, squash(state), precision=highest, preferred_element_type=jnp.float32)
            + hash_rc[step][:, None]
        )
    return state


def turns(product, modulus, sign):
    angle = sign * 2.0 * math.pi / modulus * (product % modulus).astype(jnp.float32)
    return (jnp.cos(angle), jnp.sin(angle))


def complex_mul(left_re, left_im, right_re, right_im):
    return (left_re * right_re - left_im * right_im, left_re * right_im + left_im * right_re)


def block_table(cos_t, sin_t):
    return jnp.concatenate(
        [jnp.concatenate([cos_t, -sin_t], axis=1), jnp.concatenate([sin_t, cos_t], axis=1)], axis=0
    )


def local_dft(values_re, values_im, sign):
    length = values_re.shape[-1]
    first = 128
    second = length // first
    leading = values_re.shape[:-1]
    stacked = jnp.concatenate(
        [values_re.reshape(leading + (first, second)), values_im.reshape(leading + (first, second))],
        axis=-2,
    )
    index_one = jnp.arange(first, dtype=jnp.int32)
    index_two = jnp.arange(second, dtype=jnp.int32)
    table_one = block_table(*turns(index_one[:, None] * index_one[None, :], first, sign))
    section = jnp.einsum("kn,...nm->...km", table_one, stacked, precision=three_pass)
    section_re, section_im = section[..., :first, :], section[..., first:, :]
    twist_cos, twist_sin = turns(index_one[:, None] * index_two[None, :], length, sign)
    section_re, section_im = complex_mul(section_re, section_im, twist_cos, twist_sin)
    table_two = block_table(*turns(index_two[:, None] * index_two[None, :], second, sign))
    both = jnp.concatenate([section_re, section_im], axis=-1)
    final = jnp.einsum("jn,...kn->...jk", table_two, both, precision=three_pass)
    final_re = final[..., :second, :].reshape(leading + (length,))
    final_im = final[..., second:, :].reshape(leading + (length,))
    return (final_re, final_im)


def lift_dft(values_re, values_im, sign):
    segs, phases, length = values_re.shape
    first = 128
    second = length // first
    stacked = jnp.concatenate(
        [values_re.reshape(segs, phases, first, second), values_im.reshape(segs, phases, first, second)],
        axis=2,
    )
    index_one = jnp.arange(first, dtype=jnp.int32)
    index_two = jnp.arange(second, dtype=jnp.int32)
    table_one = block_table(*turns(index_one[:, None] * index_one[None, :], first, sign))
    section = jnp.einsum("kn,spnm->skpm", table_one, stacked, precision=three_pass)
    section_re, section_im = section[:, :first], section[:, first:]
    twist_cos, twist_sin = turns(index_one[:, None] * index_two[None, :], length, sign)
    section_re, section_im = complex_mul(
        section_re, section_im, twist_cos[:, None, :], twist_sin[:, None, :]
    )
    both = jnp.concatenate([section_re, section_im], axis=-1).reshape(segs, first * phases, 2 * second)
    table_two = block_table(*turns(index_two[:, None] * index_two[None, :], second, sign))
    final = jnp.einsum("jm,sxm->sjx", table_two, both, precision=three_pass)
    final_re = final[:, :second].reshape(segs, length * phases)
    final_im = final[:, second:].reshape(segs, length * phases)
    return (final_re, final_im)


def lift_eval(coef_re, coef_im, phases, row_index, total_rows, devices):
    segs, length = coef_re.shape
    first = 128
    second = length // first
    band = length * phases
    stacked = jnp.concatenate(
        [coef_re.reshape(segs, first, second), coef_im.reshape(segs, first, second)], axis=1
    )
    index_one = jnp.arange(first, dtype=jnp.int32)
    index_two = jnp.arange(second, dtype=jnp.int32)
    index_p = jnp.arange(phases, dtype=jnp.int32)
    k_one = index_one[None, :, None]
    n_one = index_one[None, None, :]
    p_one = index_p[:, None, None]
    angle_one = (
        (k_one * n_one % first) * (total_rows // first)
        + (p_one * n_one) * (total_rows // (first * phases))
        + (phases * k_one + p_one) * row_index
    )
    cos_one, sin_one = turns(angle_one, total_rows, 1.0)
    table_one = jnp.concatenate(
        [jnp.concatenate([cos_one, -sin_one], axis=2), jnp.concatenate([sin_one, cos_one], axis=2)],
        axis=1,
    )
    section = jnp.einsum("pkn,snm->skpm", table_one, stacked, precision=three_pass)
    section_re, section_im = section[:, :first], section[:, first:]
    twist = (phases * index_one[:, None, None] + index_p[None, :, None]) * index_two[None, None, :]
    twist_cos, twist_sin = turns(twist, band, 1.0)
    section_re, section_im = complex_mul(section_re, section_im, twist_cos, twist_sin)
    both = jnp.concatenate([section_re, section_im], axis=-1).reshape(segs, first * phases, 2 * second)
    angle_two = (index_two[:, None] * index_two[None, :] % second) * (total_rows // second) + (
        index_two[:, None] * row_index * (first * phases)
    )
    cos_two, sin_two = turns(angle_two, total_rows, 1.0)
    rows_per = 2 * second // devices
    table_two = (
        jnp.stack(
            [jnp.concatenate([cos_two, -sin_two], axis=1), jnp.concatenate([sin_two, cos_two], axis=1)]
        )
        .reshape(2, devices, rows_per // 2, 2 * second)
        .transpose(1, 0, 2, 3)
        .reshape(2 * second, 2 * second)
    )
    final = jnp.einsum("jm,sxm->sjx", table_two, both, precision=three_pass)
    return final.reshape(segs, devices, rows_per, first * phases).transpose(1, 0, 2, 3)


def regroup(values):
    return lax.all_to_all(values, ("rows", "cols"), split_axis=1, concat_axis=1, tiled=True)


def column_relay(values):
    return lax.all_to_all(values, "cols", split_axis=1, concat_axis=1, tiled=True)


def on_device(trace, selectors, mds, quad, alpha, challenges, divisor_inv, hash_mds, hash_rc):
    width = trace.shape[0]
    rows_dev = trace.shape[1]
    n_rows = lax.axis_size("rows")
    n_cols = lax.axis_size("cols")
    devices = n_rows * n_cols
    total_rows = rows_dev * devices
    flat_index = lax.axis_index(("rows", "cols"))
    row_index = lax.axis_index("rows")
    rim = from_behind(trace[:, :BLOWUP], ("rows", "cols"), -1)
    extended = jnp.concatenate([trace, rim], axis=1)
    following = extended[:, BLOWUP:]
    linear = jnp.dot(mds, trace, precision=highest, preferred_element_type=jnp.float32)
    cons = following - linear - quad[:, None] * trace * trace
    step_size = challenges[0] / jnp.sqrt(jnp.float32(total_rows))
    gamma = challenges[1]
    numer = 1.0 + step_size * (extended[0] + gamma * extended[1])
    denom = 1.0 + step_size * (extended[2] + gamma * extended[3])
    ratio_log = jnp.log(numer) - jnp.log(denom)
    own_terms = ratio_log[:rows_dev]
    running_sum = jnp.cumsum(own_terms)
    offset = entering(running_sum[-1], ("rows", "cols"))
    running = jnp.exp(offset + running_sum - own_terms)
    window = own_terms
    for shift_step in range(1, BLOWUP):
        window = window + ratio_log[shift_step : shift_step + rows_dev]
    grand = running * (jnp.exp(window) * denom[:rows_dev] - numer[:rows_dev]) / step_size
    picked = selectors.astype(jnp.float32)
    combined = (
        jnp.sum(alpha[:width, None] * picked[:width] * cons, axis=0)
        + alpha[width] * picked[width] * grand
    )
    quotient = divisor_inv * combined
    parts = rows_dev // devices
    gathered = regroup(quotient.reshape(1, rows_dev)).reshape(devices, parts)
    block_index = jnp.arange(devices, dtype=jnp.int32)
    cos_block, sin_block = turns(block_index[:, None] * block_index[None, :], devices, -1.0)
    first_re = jnp.dot(cos_block, gathered, precision=three_pass, preferred_element_type=jnp.float32)
    first_im = jnp.dot(sin_block, gathered, precision=three_pass, preferred_element_type=jnp.float32)
    global_pos = flat_index * parts + jnp.arange(parts, dtype=jnp.int32)
    twist_cos, twist_sin = turns(block_index[:, None] * global_pos[None, :], total_rows, -1.0)
    first_re, first_im = complex_mul(first_re, first_im, twist_cos, twist_sin)
    ordered = (
        jnp.stack([first_re, first_im])
        .reshape(2, n_cols, n_rows, parts)
        .transpose(0, 2, 1, 3)
        .reshape(2, devices * parts)
    )
    columns = regroup(ordered)
    coef_re, coef_im = local_dft(columns[0], columns[1], -1.0)
    coef_re = coef_re / total_rows
    coef_im = coef_im / total_rows
    seg_dev = SEGMENTS // n_cols
    seg_rows = rows_dev // SEGMENTS
    packed = jnp.stack([coef_re, coef_im]).reshape(2, n_cols, seg_dev, seg_rows)
    owned = column_relay(packed)
    owned = owned.transpose(0, 2, 3, 1).reshape(2, seg_dev, seg_rows * n_cols)
    short = seg_rows * n_cols
    band = short * SEGMENTS
    small = band // devices
    lifted = lift_eval(owned[0], owned[1], SEGMENTS, row_index, total_rows, devices)
    arrived = lax.all_to_all(lifted, ("rows", "cols"), 0, 0, tiled=True)
    arrived = arrived.reshape(n_rows, n_cols, seg_dev, 2, -1, lifted.shape[-1])
    arrived_re, arrived_im = arrived[:, :, :, 0], arrived[:, :, :, 1]
    row_ids = jnp.arange(n_rows, dtype=jnp.int32)
    cos_rows, sin_rows = turns(row_ids[:, None] * row_ids[None, :], n_rows, 1.0)
    summed_re = jnp.einsum("ab,bcsvu->csavu", cos_rows, arrived_re, precision=three_pass) - jnp.einsum(
        "ab,bcsvu->csavu", sin_rows, arrived_im, precision=three_pass
    )
    summed_im = jnp.einsum("ab,bcsvu->csavu", sin_rows, arrived_re, precision=three_pass) + jnp.einsum(
        "ab,bcsvu->csavu", cos_rows, arrived_im, precision=three_pass
    )
    values = jnp.stack([summed_re, summed_im]).reshape(2, SEGMENTS, n_rows, small)
    leaf_count = n_rows * small
    real_part = values[0].reshape(SEGMENTS, leaf_count)
    imag_part = values[1].reshape(SEGMENTS, leaf_count)
    zeros = jnp.zeros((DIGEST, leaf_count), jnp.float32)
    state = permute(jnp.concatenate([zeros, real_part], axis=0), hash_mds, hash_rc)
    state = state + jnp.concatenate([zeros, imag_part], axis=0)
    state = permute(state, hash_mds, hash_rc)
    return state[:DIGEST].reshape(DIGEST, n_rows, small)


def solution(mesh):
    in_specs = (
        P(None, ("rows", "cols")),
        P(None, ("rows", "cols")),
        P(),
        P(),
        P(),
        P(),
        P(("rows", "cols")),
        P(),
        P(),
    )
    out_specs = P(None, None, ("rows", "cols"))
    return jax.shard_map(
        on_device, mesh=mesh, in_specs=in_specs, out_specs=out_specs, check_vma=False
    )
```

```python
import math

import jax
import jax.numpy as jnp
from jax import lax
from jax.sharding import PartitionSpec as P

BLOWUP = 8
SEGMENTS = 8
DIGEST = 4
ROUNDS = 2


highest = lax.Precision.HIGHEST
three_pass = lax.Precision.HIGH


def from_behind(array, axis, by):
    count = lax.axis_size(axis)
    return lax.ppermute(array, axis, [(i, (i + by) % count) for i in range(count)])


def entering(value, axis):
    count, mine = (lax.axis_size(axis), lax.axis_index(axis))
    spread = jnp.broadcast_to(value, (count,))
    pieces = lax.all_to_all(spread, axis, 0, 0, tiled=True)
    earlier = jnp.arange(count, dtype=jnp.int32) < mine
    return jnp.sum(jnp.where(earlier, pieces, jnp.zeros_like(pieces)))


def squash(value):
    return value * lax.rsqrt(1.0 + value * value)


def permute(state, hash_mds, hash_rc):
    for step in range(ROUNDS):
        state = (
            jnp.dot(hash_mds, squash(state), precision=highest, preferred_element_type=jnp.float32)
            + hash_rc[step][:, None]
        )
    return state


def turns(product, modulus, sign):
    angle = sign * 2.0 * math.pi / modulus * (product % modulus).astype(jnp.float32)
    return (jnp.cos(angle), jnp.sin(angle))


def complex_mul(left_re, left_im, right_re, right_im):
    return (left_re * right_re - left_im * right_im, left_re * right_im + left_im * right_re)


def block_table(cos_t, sin_t):
    return jnp.concatenate(
        [jnp.concatenate([cos_t, -sin_t], axis=1), jnp.concatenate([sin_t, cos_t], axis=1)], axis=0
    )


def local_dft(values_re, values_im, sign):
    length = values_re.shape[-1]
    first = 128
    second = length // first
    leading = values_re.shape[:-1]
    stacked = jnp.concatenate(
        [values_re.reshape(leading + (first, second)), values_im.reshape(leading + (first, second))],
        axis=-2,
    )
    index_one = jnp.arange(first, dtype=jnp.int32)
    index_two = jnp.arange(second, dtype=jnp.int32)
    table_one = block_table(*turns(index_one[:, None] * index_one[None, :], first, sign))
    section = jnp.einsum("kn,...nm->...km", table_one, stacked, precision=three_pass)
    section_re, section_im = section[..., :first, :], section[..., first:, :]
    twist_cos, twist_sin = turns(index_one[:, None] * index_two[None, :], length, sign)
    section_re, section_im = complex_mul(section_re, section_im, twist_cos, twist_sin)
    table_two = block_table(*turns(index_two[:, None] * index_two[None, :], second, sign))
    both = jnp.concatenate([section_re, section_im], axis=-1)
    final = jnp.einsum("jn,...kn->...jk", table_two, both, precision=three_pass)
    final_re = final[..., :second, :].reshape(leading + (length,))
    final_im = final[..., second:, :].reshape(leading + (length,))
    return (final_re, final_im)


def lift_dft(values_re, values_im, sign):
    segs, phases, length = values_re.shape
    first = 128
    second = length // first
    stacked = jnp.concatenate(
        [values_re.reshape(segs, phases, first, second), values_im.reshape(segs, phases, first, second)],
        axis=2,
    )
    index_one = jnp.arange(first, dtype=jnp.int32)
    index_two = jnp.arange(second, dtype=jnp.int32)
    table_one = block_table(*turns(index_one[:, None] * index_one[None, :], first, sign))
    section = jnp.einsum("kn,spnm->skpm", table_one, stacked, precision=three_pass)
    section_re, section_im = section[:, :first], section[:, first:]
    twist_cos, twist_sin = turns(index_one[:, None] * index_two[None, :], length, sign)
    section_re, section_im = complex_mul(
        section_re, section_im, twist_cos[:, None, :], twist_sin[:, None, :]
    )
    both = jnp.concatenate([section_re, section_im], axis=-1).reshape(segs, first * phases, 2 * second)
    table_two = block_table(*turns(index_two[:, None] * index_two[None, :], second, sign))
    final = jnp.einsum("jm,sxm->sjx", table_two, both, precision=three_pass)
    final_re = final[:, :second].reshape(segs, length * phases)
    final_im = final[:, second:].reshape(segs, length * phases)
    return (final_re, final_im)


def lift_eval(coef_re, coef_im, phases, row_index, total_rows, devices):
    segs, length = coef_re.shape
    first = 128
    second = length // first
    band = length * phases
    stacked = jnp.concatenate(
        [coef_re.reshape(segs, first, second), coef_im.reshape(segs, first, second)], axis=1
    )
    index_one = jnp.arange(first, dtype=jnp.int32)
    index_two = jnp.arange(second, dtype=jnp.int32)
    index_p = jnp.arange(phases, dtype=jnp.int32)
    k_one = index_one[None, :, None]
    n_one = index_one[None, None, :]
    p_one = index_p[:, None, None]
    angle_one = (
        (k_one * n_one % first) * (total_rows // first)
        + (p_one * n_one) * (total_rows // (first * phases))
        + (phases * k_one + p_one) * row_index
    )
    cos_one, sin_one = turns(angle_one, total_rows, 1.0)
    table_one = jnp.concatenate(
        [jnp.concatenate([cos_one, -sin_one], axis=2), jnp.concatenate([sin_one, cos_one], axis=2)],
        axis=1,
    )
    section = jnp.einsum("pkn,snm->skpm", table_one, stacked, precision=three_pass)
    section_re, section_im = section[:, :first], section[:, first:]
    twist = (phases * index_one[:, None, None] + index_p[None, :, None]) * index_two[None, None, :]
    twist_cos, twist_sin = turns(twist, band, 1.0)
    section_re, section_im = complex_mul(section_re, section_im, twist_cos, twist_sin)
    both = jnp.concatenate([section_re, section_im], axis=-1).reshape(segs, first * phases, 2 * second)
    angle_two = (index_two[:, None] * index_two[None, :] % second) * (total_rows // second) + (
        index_two[:, None] * row_index * (first * phases)
    )
    cos_two, sin_two = turns(angle_two, total_rows, 1.0)
    rows_per = 2 * second // devices
    table_two = (
        jnp.stack(
            [jnp.concatenate([cos_two, -sin_two], axis=1), jnp.concatenate([sin_two, cos_two], axis=1)]
        )
        .reshape(2, devices, rows_per // 2, 2 * second)
        .transpose(1, 0, 2, 3)
        .reshape(2 * second, 2 * second)
    )
    final = jnp.einsum("jm,sxm->sjx", table_two, both, precision=three_pass)
    return final.reshape(segs, devices, rows_per, first * phases).transpose(1, 0, 2, 3)


def regroup(values):
    return lax.all_to_all(values, ("rows", "cols"), split_axis=1, concat_axis=1, tiled=True)


def column_relay(values):
    return lax.all_to_all(values, "cols", split_axis=1, concat_axis=1, tiled=True)


def on_device(trace, selectors, mds, quad, alpha, challenges, divisor_inv, hash_mds, hash_rc):
    width = trace.shape[0]
    rows_dev = trace.shape[1]
    n_rows = lax.axis_size("rows")
    n_cols = lax.axis_size("cols")
    devices = n_rows * n_cols
    total_rows = rows_dev * devices
    flat_index = lax.axis_index(("rows", "cols"))
    row_index = lax.axis_index("rows")
    rim = from_behind(trace[:, :BLOWUP], ("rows", "cols"), -1)
    extended = jnp.concatenate([trace, rim], axis=1)
    following = extended[:, BLOWUP:]
    linear = jnp.dot(mds, trace, precision=highest, preferred_element_type=jnp.float32)
    cons = following - linear - quad[:, None] * trace * trace
    step_size = challenges[0] / jnp.sqrt(jnp.float32(total_rows))
    gamma = challenges[1]
    numer = 1.0 + step_size * (extended[0] + gamma * extended[1])
    denom = 1.0 + step_size * (extended[2] + gamma * extended[3])
    ratio_log = jnp.log(numer) - jnp.log(denom)
    own_terms = ratio_log[:rows_dev]
    running_sum = jnp.cumsum(own_terms)
    offset = entering(running_sum[-1], ("rows", "cols"))
    running = jnp.exp(offset + running_sum - own_terms)
    window = own_terms
    for shift_step in range(1, BLOWUP):
        window = window + ratio_log[shift_step : shift_step + rows_dev]
    grand = running * (jnp.exp(window) * denom[:rows_dev] - numer[:rows_dev]) / step_size
    chosen = selectors != 0
    terms = jnp.where(chosen[:width], alpha[:width, None] * cons, jnp.zeros_like(cons))
    combined = jnp.sum(terms, axis=0) + jnp.where(
        chosen[width], alpha[width] * grand, jnp.zeros_like(grand)
    )
    quotient = divisor_inv * combined
    parts = rows_dev // devices
    gathered = regroup(quotient.reshape(1, rows_dev)).reshape(devices, parts)
    block_index = jnp.arange(devices, dtype=jnp.int32)
    cos_block, sin_block = turns(block_index[:, None] * block_index[None, :], devices, -1.0)
    first_re = jnp.dot(cos_block, gathered, precision=three_pass, preferred_element_type=jnp.float32)
    first_im = jnp.dot(sin_block, gathered, precision=three_pass, preferred_element_type=jnp.float32)
    global_pos = flat_index * parts + jnp.arange(parts, dtype=jnp.int32)
    twist_cos, twist_sin = turns(block_index[:, None] * global_pos[None, :], total_rows, -1.0)
    first_re, first_im = complex_mul(first_re, first_im, twist_cos, twist_sin)
    ordered = (
        jnp.stack([first_re, first_im])
        .reshape(2, n_cols, n_rows, parts)
        .transpose(0, 2, 1, 3)
        .reshape(2, devices * parts)
    )
    columns = regroup(ordered)
    coef_re, coef_im = local_dft(columns[0], columns[1], -1.0)
    coef_re = coef_re / total_rows
    coef_im = coef_im / total_rows
    seg_dev = SEGMENTS // n_cols
    seg_rows = rows_dev // SEGMENTS
    packed = jnp.stack([coef_re, coef_im]).reshape(2, n_cols, seg_dev, seg_rows)
    owned = column_relay(packed)
    owned = owned.transpose(0, 2, 3, 1).reshape(2, seg_dev, seg_rows * n_cols)
    short = seg_rows * n_cols
    band = short * SEGMENTS
    small = band // devices
    lifted = lift_eval(owned[0], owned[1], SEGMENTS, row_index, total_rows, devices)
    arrived = lax.all_to_all(lifted, ("rows", "cols"), 0, 0, tiled=True)
    arrived = arrived.reshape(n_rows, n_cols, seg_dev, 2, -1, lifted.shape[-1])
    arrived_re, arrived_im = arrived[:, :, :, 0], arrived[:, :, :, 1]
    row_ids = jnp.arange(n_rows, dtype=jnp.int32)
    cos_rows, sin_rows = turns(row_ids[:, None] * row_ids[None, :], n_rows, 1.0)
    summed_re = jnp.einsum("ab,bcsvu->csavu", cos_rows, arrived_re, precision=three_pass) - jnp.einsum(
        "ab,bcsvu->csavu", sin_rows, arrived_im, precision=three_pass
    )
    summed_im = jnp.einsum("ab,bcsvu->csavu", sin_rows, arrived_re, precision=three_pass) + jnp.einsum(
        "ab,bcsvu->csavu", cos_rows, arrived_im, precision=three_pass
    )
    values = jnp.stack([summed_re, summed_im]).reshape(2, SEGMENTS, n_rows, small)
    leaf_count = n_rows * small
    real_part = values[0].reshape(SEGMENTS, leaf_count)
    imag_part = values[1].reshape(SEGMENTS, leaf_count)
    zeros = jnp.zeros((DIGEST, leaf_count), jnp.float32)
    state = permute(jnp.concatenate([zeros, real_part], axis=0), hash_mds, hash_rc)
    state = state + jnp.concatenate([zeros, imag_part], axis=0)
    state = permute(state, hash_mds, hash_rc)
    return state[:DIGEST].reshape(DIGEST, n_rows, small)


def solution(mesh):
    in_specs = (
        P(None, ("rows", "cols")),
        P(None, ("rows", "cols")),
        P(),
        P(),
        P(),
        P(),
        P(("rows", "cols")),
        P(),
        P(),
    )
    out_specs = P(None, None, ("rows", "cols"))
    return jax.shard_map(
        on_device, mesh=mesh, in_specs=in_specs, out_specs=out_specs, check_vma=False
    )
```

```python
import math

import jax
import jax.numpy as jnp
from jax import lax
from jax.sharding import PartitionSpec as P

BLOWUP = 8
SEGMENTS = 8
DIGEST = 4
ROUNDS = 2


highest = lax.Precision.HIGHEST
three_pass = lax.Precision.HIGH


def from_behind(array, axis, by):
    count = lax.axis_size(axis)
    return lax.ppermute(array, axis, [(i, (i + by) % count) for i in range(count)])


def entering(value, axis):
    count, mine = (lax.axis_size(axis), lax.axis_index(axis))
    spread = jnp.broadcast_to(value, (count,))
    pieces = lax.all_to_all(spread, axis, 0, 0, tiled=True)
    earlier = jnp.arange(count, dtype=jnp.int32) < mine
    return jnp.sum(jnp.where(earlier, pieces, jnp.zeros_like(pieces)))


def squash(value):
    return value * lax.rsqrt(1.0 + value * value)


def permute(state, hash_mds, hash_rc):
    for step in range(ROUNDS):
        state = (
            jnp.dot(hash_mds, squash(state), precision=highest, preferred_element_type=jnp.float32)
            + hash_rc[step][:, None]
        )
    return state


def turns(product, modulus, sign):
    angle = sign * 2.0 * math.pi / modulus * (product % modulus).astype(jnp.float32)
    return (jnp.cos(angle), jnp.sin(angle))


def complex_mul(left_re, left_im, right_re, right_im):
    return (left_re * right_re - left_im * right_im, left_re * right_im + left_im * right_re)


def block_table(cos_t, sin_t):
    return jnp.concatenate(
        [jnp.concatenate([cos_t, -sin_t], axis=1), jnp.concatenate([sin_t, cos_t], axis=1)], axis=0
    )


def local_dft(values_re, values_im, sign):
    length = values_re.shape[-1]
    first = 128
    second = length // first
    leading = values_re.shape[:-1]
    stacked = jnp.concatenate(
        [values_re.reshape(leading + (first, second)), values_im.reshape(leading + (first, second))],
        axis=-2,
    )
    index_one = jnp.arange(first, dtype=jnp.int32)
    index_two = jnp.arange(second, dtype=jnp.int32)
    table_one = block_table(*turns(index_one[:, None] * index_one[None, :], first, sign))
    section = jnp.einsum("kn,...nm->...km", table_one, stacked, precision=three_pass)
    section_re, section_im = section[..., :first, :], section[..., first:, :]
    twist_cos, twist_sin = turns(index_one[:, None] * index_two[None, :], length, sign)
    section_re, section_im = complex_mul(section_re, section_im, twist_cos, twist_sin)
    table_two = block_table(*turns(index_two[:, None] * index_two[None, :], second, sign))
    both = jnp.concatenate([section_re, section_im], axis=-1)
    final = jnp.einsum("jn,...kn->...jk", table_two, both, precision=three_pass)
    final_re = final[..., :second, :].reshape(leading + (length,))
    final_im = final[..., second:, :].reshape(leading + (length,))
    return (final_re, final_im)


def lift_dft(values_re, values_im, sign):
    segs, phases, length = values_re.shape
    first = 128
    second = length // first
    stacked = jnp.concatenate(
        [values_re.reshape(segs, phases, first, second), values_im.reshape(segs, phases, first, second)],
        axis=2,
    )
    index_one = jnp.arange(first, dtype=jnp.int32)
    index_two = jnp.arange(second, dtype=jnp.int32)
    table_one = block_table(*turns(index_one[:, None] * index_one[None, :], first, sign))
    section = jnp.einsum("kn,spnm->skpm", table_one, stacked, precision=three_pass)
    section_re, section_im = section[:, :first], section[:, first:]
    twist_cos, twist_sin = turns(index_one[:, None] * index_two[None, :], length, sign)
    section_re, section_im = complex_mul(
        section_re, section_im, twist_cos[:, None, :], twist_sin[:, None, :]
    )
    both = jnp.concatenate([section_re, section_im], axis=-1).reshape(segs, first * phases, 2 * second)
    table_two = block_table(*turns(index_two[:, None] * index_two[None, :], second, sign))
    final = jnp.einsum("jm,sxm->sjx", table_two, both, precision=three_pass)
    final_re = final[:, :second].reshape(segs, length * phases)
    final_im = final[:, second:].reshape(segs, length * phases)
    return (final_re, final_im)


def lift_eval(coef_re, coef_im, phases, row_index, total_rows, devices):
    segs, length = coef_re.shape
    first = 128
    second = length // first
    band = length * phases
    stacked = jnp.concatenate(
        [coef_re.reshape(segs, first, second), coef_im.reshape(segs, first, second)], axis=1
    )
    index_one = jnp.arange(first, dtype=jnp.int32)
    index_two = jnp.arange(second, dtype=jnp.int32)
    index_p = jnp.arange(phases, dtype=jnp.int32)
    k_one = index_one[None, :, None]
    n_one = index_one[None, None, :]
    p_one = index_p[:, None, None]
    angle_one = (
        (k_one * n_one % first) * (total_rows // first)
        + (p_one * n_one) * (total_rows // (first * phases))
        + (phases * k_one + p_one) * row_index
    )
    cos_one, sin_one = turns(angle_one, total_rows, 1.0)
    table_one = jnp.concatenate(
        [jnp.concatenate([cos_one, -sin_one], axis=2), jnp.concatenate([sin_one, cos_one], axis=2)],
        axis=1,
    )
    section = jnp.einsum("pkn,snm->skpm", table_one, stacked, precision=three_pass)
    section_re, section_im = section[:, :first], section[:, first:]
    twist = (phases * index_one[:, None, None] + index_p[None, :, None]) * index_two[None, None, :]
    twist_cos, twist_sin = turns(twist, band, 1.0)
    section_re, section_im = complex_mul(section_re, section_im, twist_cos, twist_sin)
    both = jnp.concatenate([section_re, section_im], axis=-1).reshape(segs, first * phases, 2 * second)
    angle_two = (index_two[:, None] * index_two[None, :] % second) * (total_rows // second) + (
        index_two[:, None] * row_index * (first * phases)
    )
    cos_two, sin_two = turns(angle_two, total_rows, 1.0)
    rows_per = 2 * second // devices
    table_two = (
        jnp.stack(
            [jnp.concatenate([cos_two, -sin_two], axis=1), jnp.concatenate([sin_two, cos_two], axis=1)]
        )
        .reshape(2, devices, rows_per // 2, 2 * second)
        .transpose(1, 0, 2, 3)
        .reshape(2 * second, 2 * second)
    )
    final = jnp.einsum("jm,sxm->sjx", table_two, both, precision=three_pass)
    return final.reshape(segs, devices, rows_per, first * phases).transpose(1, 0, 2, 3)


def regroup(values):
    return lax.all_to_all(values, ("rows", "cols"), split_axis=1, concat_axis=1, tiled=True)


def column_relay(values):
    return lax.all_to_all(values, "cols", split_axis=1, concat_axis=1, tiled=True)


def on_device(trace, selectors, mds, quad, alpha, challenges, divisor_inv, hash_mds, hash_rc):
    width = trace.shape[0]
    rows_dev = trace.shape[1]
    n_rows = lax.axis_size("rows")
    n_cols = lax.axis_size("cols")
    devices = n_rows * n_cols
    total_rows = rows_dev * devices
    flat_index = lax.axis_index(("rows", "cols"))
    row_index = lax.axis_index("rows")
    rim = from_behind(trace[:, :BLOWUP], ("rows", "cols"), -1)
    extended = jnp.concatenate([trace, rim], axis=1)
    following = extended[:, BLOWUP:]
    linear = jnp.dot(mds, trace, precision=highest, preferred_element_type=jnp.float32)
    cons = following - linear - quad[:, None] * trace * trace
    step_size = challenges[0] / jnp.sqrt(jnp.float32(total_rows))
    gamma = challenges[1]
    numer = 1.0 + step_size * (extended[0] + gamma * extended[1])
    denom = 1.0 + step_size * (extended[2] + gamma * extended[3])
    ratio_log = jnp.log(numer) - jnp.log(denom)
    own_terms = ratio_log[:rows_dev]
    running_sum = jnp.cumsum(own_terms)
    offset = entering(running_sum[-1], ("rows", "cols"))
    running = jnp.exp(offset + running_sum - own_terms)
    window = own_terms
    for shift_step in range(1, BLOWUP):
        window = window + ratio_log[shift_step : shift_step + rows_dev]
    grand = running * (jnp.exp(window) * denom[:rows_dev] - numer[:rows_dev]) / step_size
    picked = selectors.astype(jnp.float32)
    combined = (
        jnp.sum(alpha[:width, None] * picked[:width] * cons, axis=0)
        + alpha[width] * picked[width] * grand
    )
    quotient = divisor_inv * combined
    parts = rows_dev // devices
    gathered = regroup(quotient.reshape(1, rows_dev)).reshape(devices, parts)
    block_index = jnp.arange(devices, dtype=jnp.int32)
    cos_block, sin_block = turns(block_index[:, None] * block_index[None, :], devices, -1.0)
    first_re = jnp.dot(cos_block, gathered, precision=three_pass, preferred_element_type=jnp.float32)
    first_im = jnp.dot(sin_block, gathered, precision=three_pass, preferred_element_type=jnp.float32)
    global_pos = flat_index * parts + jnp.arange(parts, dtype=jnp.int32)
    twist_cos, twist_sin = turns(block_index[:, None] * global_pos[None, :], total_rows, -1.0)
    first_re, first_im = complex_mul(first_re, first_im, twist_cos, twist_sin)
    ordered = (
        jnp.stack([first_re, first_im])
        .reshape(2, n_cols, n_rows, parts)
        .transpose(0, 2, 1, 3)
        .reshape(2, devices * parts)
    )
    columns = regroup(ordered)
    coef_re, coef_im = local_dft(columns[0], columns[1], -1.0)
    coef_re = coef_re / total_rows
    coef_im = coef_im / total_rows
    seg_dev = SEGMENTS // n_cols
    seg_rows = rows_dev // SEGMENTS
    packed = jnp.stack([coef_re, coef_im]).reshape(2, n_cols, seg_dev, seg_rows)
    owned = column_relay(packed)
    owned = owned.transpose(0, 2, 3, 1).reshape(2, seg_dev, seg_rows * n_cols)
    short = seg_rows * n_cols
    band = short * SEGMENTS
    small = band // devices
    lifted = lift_eval(owned[0], owned[1], SEGMENTS, row_index, total_rows, devices)
    arrived = lax.all_to_all(lifted, ("rows", "cols"), 0, 0, tiled=True)
    arrived = arrived.reshape(n_rows, n_cols, seg_dev, 2, -1, lifted.shape[-1])
    row_ids = jnp.arange(n_rows, dtype=jnp.int32)
    cos_rows, sin_rows = turns(row_ids[:, None] * row_ids[None, :], n_rows, 1.0)
    table_rows = jnp.stack(
        [jnp.stack([cos_rows, -sin_rows], axis=1), jnp.stack([sin_rows, cos_rows], axis=1)]
    )
    values = jnp.einsum("Rarb,bcsrvu->Rcsavu", table_rows, arrived, precision=three_pass).reshape(
        2, SEGMENTS, n_rows, small
    )
    leaf_count = n_rows * small
    real_part = values[0].reshape(SEGMENTS, leaf_count)
    imag_part = values[1].reshape(SEGMENTS, leaf_count)
    zeros = jnp.zeros((DIGEST, leaf_count), jnp.float32)
    state = permute(jnp.concatenate([zeros, real_part], axis=0), hash_mds, hash_rc)
    state = state + jnp.concatenate([zeros, imag_part], axis=0)
    state = permute(state, hash_mds, hash_rc)
    return state[:DIGEST].reshape(DIGEST, n_rows, small)


def solution(mesh):
    in_specs = (
        P(None, ("rows", "cols")),
        P(None, ("rows", "cols")),
        P(),
        P(),
        P(),
        P(),
        P(("rows", "cols")),
        P(),
        P(),
    )
    out_specs = P(None, None, ("rows", "cols"))
    return jax.shard_map(
        on_device, mesh=mesh, in_specs=in_specs, out_specs=out_specs, check_vma=False
    )
```

```python
import math

import jax
import jax.numpy as jnp
from jax import lax
from jax.sharding import PartitionSpec as P

BLOWUP = 8
SEGMENTS = 8
DIGEST = 4
ROUNDS = 2


highest = lax.Precision.HIGHEST
three_pass = lax.Precision.HIGH


def from_behind(array, axis, by):
    count = lax.axis_size(axis)
    return lax.ppermute(array, axis, [(i, (i + by) % count) for i in range(count)])


def entering(value, axis):
    count, mine = (lax.axis_size(axis), lax.axis_index(axis))
    spread = jnp.broadcast_to(value, (count,))
    pieces = lax.all_to_all(spread, axis, 0, 0, tiled=True)
    earlier = jnp.arange(count, dtype=jnp.int32) < mine
    return jnp.sum(jnp.where(earlier, pieces, jnp.zeros_like(pieces)))


def squash(value):
    return value * lax.rsqrt(1.0 + value * value)


def permute(state, hash_mds, hash_rc):
    for step in range(ROUNDS):
        state = (
            jnp.dot(hash_mds, squash(state), precision=three_pass, preferred_element_type=jnp.float32)
            + hash_rc[step][:, None]
        )
    return state


def turns(product, modulus, sign):
    angle = sign * 2.0 * math.pi / modulus * (product % modulus).astype(jnp.float32)
    return (jnp.cos(angle), jnp.sin(angle))


def complex_mul(left_re, left_im, right_re, right_im):
    return (left_re * right_re - left_im * right_im, left_re * right_im + left_im * right_re)


def block_table(cos_t, sin_t):
    return jnp.concatenate(
        [jnp.concatenate([cos_t, -sin_t], axis=1), jnp.concatenate([sin_t, cos_t], axis=1)], axis=0
    )


def local_dft(values_re, values_im, sign):
    length = values_re.shape[-1]
    first = 128
    second = length // first
    leading = values_re.shape[:-1]
    stacked = jnp.concatenate(
        [values_re.reshape(leading + (first, second)), values_im.reshape(leading + (first, second))],
        axis=-2,
    )
    index_one = jnp.arange(first, dtype=jnp.int32)
    index_two = jnp.arange(second, dtype=jnp.int32)
    table_one = block_table(*turns(index_one[:, None] * index_one[None, :], first, sign))
    section = jnp.einsum("kn,...nm->...km", table_one, stacked, precision=three_pass)
    section_re, section_im = section[..., :first, :], section[..., first:, :]
    twist_cos, twist_sin = turns(index_one[:, None] * index_two[None, :], length, sign)
    section_re, section_im = complex_mul(section_re, section_im, twist_cos, twist_sin)
    table_two = block_table(*turns(index_two[:, None] * index_two[None, :], second, sign))
    both = jnp.concatenate([section_re, section_im], axis=-1)
    final = jnp.einsum("jn,...kn->...jk", table_two, both, precision=three_pass)
    final_re = final[..., :second, :].reshape(leading + (length,))
    final_im = final[..., second:, :].reshape(leading + (length,))
    return (final_re, final_im)


def lift_dft(values_re, values_im, sign):
    segs, phases, length = values_re.shape
    first = 128
    second = length // first
    stacked = jnp.concatenate(
        [values_re.reshape(segs, phases, first, second), values_im.reshape(segs, phases, first, second)],
        axis=2,
    )
    index_one = jnp.arange(first, dtype=jnp.int32)
    index_two = jnp.arange(second, dtype=jnp.int32)
    table_one = block_table(*turns(index_one[:, None] * index_one[None, :], first, sign))
    section = jnp.einsum("kn,spnm->skpm", table_one, stacked, precision=three_pass)
    section_re, section_im = section[:, :first], section[:, first:]
    twist_cos, twist_sin = turns(index_one[:, None] * index_two[None, :], length, sign)
    section_re, section_im = complex_mul(
        section_re, section_im, twist_cos[:, None, :], twist_sin[:, None, :]
    )
    both = jnp.concatenate([section_re, section_im], axis=-1).reshape(segs, first * phases, 2 * second)
    table_two = block_table(*turns(index_two[:, None] * index_two[None, :], second, sign))
    final = jnp.einsum("jm,sxm->sjx", table_two, both, precision=three_pass)
    final_re = final[:, :second].reshape(segs, length * phases)
    final_im = final[:, second:].reshape(segs, length * phases)
    return (final_re, final_im)


def lift_eval(coef_re, coef_im, phases, row_index, total_rows, devices):
    segs, length = coef_re.shape
    first = 128
    second = length // first
    band = length * phases
    stacked = jnp.concatenate(
        [coef_re.reshape(segs, first, second), coef_im.reshape(segs, first, second)], axis=1
    )
    index_one = jnp.arange(first, dtype=jnp.int32)
    index_two = jnp.arange(second, dtype=jnp.int32)
    index_p = jnp.arange(phases, dtype=jnp.int32)
    k_one = index_one[None, :, None]
    n_one = index_one[None, None, :]
    p_one = index_p[:, None, None]
    angle_one = (
        (k_one * n_one % first) * (total_rows // first)
        + (p_one * n_one) * (total_rows // (first * phases))
        + (phases * k_one + p_one) * row_index
    )
    cos_one, sin_one = turns(angle_one, total_rows, 1.0)
    table_one = jnp.concatenate(
        [jnp.concatenate([cos_one, -sin_one], axis=2), jnp.concatenate([sin_one, cos_one], axis=2)],
        axis=1,
    )
    section = jnp.einsum("pkn,snm->skpm", table_one, stacked, precision=three_pass)
    section_re, section_im = section[:, :first], section[:, first:]
    twist = (phases * index_one[:, None, None] + index_p[None, :, None]) * index_two[None, None, :]
    twist_cos, twist_sin = turns(twist, band, 1.0)
    section_re, section_im = complex_mul(section_re, section_im, twist_cos, twist_sin)
    both = jnp.concatenate([section_re, section_im], axis=-1).reshape(segs, first * phases, 2 * second)
    angle_two = (index_two[:, None] * index_two[None, :] % second) * (total_rows // second) + (
        index_two[:, None] * row_index * (first * phases)
    )
    cos_two, sin_two = turns(angle_two, total_rows, 1.0)
    rows_per = 2 * second // devices
    table_two = (
        jnp.stack(
            [jnp.concatenate([cos_two, -sin_two], axis=1), jnp.concatenate([sin_two, cos_two], axis=1)]
        )
        .reshape(2, devices, rows_per // 2, 2 * second)
        .transpose(1, 0, 2, 3)
        .reshape(2 * second, 2 * second)
    )
    final = jnp.einsum("jm,sxm->sjx", table_two, both, precision=three_pass)
    return final.reshape(segs, devices, rows_per, first * phases).transpose(1, 0, 2, 3)


def regroup(values):
    return lax.all_to_all(values, ("rows", "cols"), split_axis=1, concat_axis=1, tiled=True)


def column_relay(values):
    return lax.all_to_all(values, "cols", split_axis=1, concat_axis=1, tiled=True)


def on_device(trace, selectors, mds, quad, alpha, challenges, divisor_inv, hash_mds, hash_rc):
    width = trace.shape[0]
    rows_dev = trace.shape[1]
    n_rows = lax.axis_size("rows")
    n_cols = lax.axis_size("cols")
    devices = n_rows * n_cols
    total_rows = rows_dev * devices
    flat_index = lax.axis_index(("rows", "cols"))
    row_index = lax.axis_index("rows")
    rim = from_behind(trace[:, :BLOWUP], ("rows", "cols"), -1)
    extended = jnp.concatenate([trace, rim], axis=1)
    following = extended[:, BLOWUP:]
    linear = jnp.dot(mds, trace, precision=highest, preferred_element_type=jnp.float32)
    cons = following - linear - quad[:, None] * trace * trace
    step_size = challenges[0] / jnp.sqrt(jnp.float32(total_rows))
    gamma = challenges[1]
    numer = 1.0 + step_size * (extended[0] + gamma * extended[1])
    denom = 1.0 + step_size * (extended[2] + gamma * extended[3])
    ratio_log = jnp.log(numer) - jnp.log(denom)
    own_terms = ratio_log[:rows_dev]
    running_sum = jnp.cumsum(own_terms)
    offset = entering(running_sum[-1], ("rows", "cols"))
    running = jnp.exp(offset + running_sum - own_terms)
    window = own_terms
    for shift_step in range(1, BLOWUP):
        window = window + ratio_log[shift_step : shift_step + rows_dev]
    grand = running * (jnp.exp(window) * denom[:rows_dev] - numer[:rows_dev]) / step_size
    picked = selectors.astype(jnp.float32)
    combined = (
        jnp.sum(alpha[:width, None] * picked[:width] * cons, axis=0)
        + alpha[width] * picked[width] * grand
    )
    quotient = divisor_inv * combined
    parts = rows_dev // devices
    gathered = regroup(quotient.reshape(1, rows_dev)).reshape(devices, parts)
    block_index = jnp.arange(devices, dtype=jnp.int32)
    cos_block, sin_block = turns(block_index[:, None] * block_index[None, :], devices, -1.0)
    first_re = jnp.dot(cos_block, gathered, precision=three_pass, preferred_element_type=jnp.float32)
    first_im = jnp.dot(sin_block, gathered, precision=three_pass, preferred_element_type=jnp.float32)
    global_pos = flat_index * parts + jnp.arange(parts, dtype=jnp.int32)
    twist_cos, twist_sin = turns(block_index[:, None] * global_pos[None, :], total_rows, -1.0)
    first_re, first_im = complex_mul(first_re, first_im, twist_cos, twist_sin)
    ordered = (
        jnp.stack([first_re, first_im])
        .reshape(2, n_cols, n_rows, parts)
        .transpose(0, 2, 1, 3)
        .reshape(2, devices * parts)
    )
    columns = regroup(ordered)
    coef_re, coef_im = local_dft(columns[0], columns[1], -1.0)
    coef_re = coef_re / total_rows
    coef_im = coef_im / total_rows
    seg_dev = SEGMENTS // n_cols
    seg_rows = rows_dev // SEGMENTS
    packed = jnp.stack([coef_re, coef_im]).reshape(2, n_cols, seg_dev, seg_rows)
    owned = column_relay(packed)
    owned = owned.transpose(0, 2, 3, 1).reshape(2, seg_dev, seg_rows * n_cols)
    short = seg_rows * n_cols
    band = short * SEGMENTS
    small = band // devices
    lifted = lift_eval(owned[0], owned[1], SEGMENTS, row_index, total_rows, devices)
    arrived = lax.all_to_all(lifted, ("rows", "cols"), 0, 0, tiled=True)
    arrived = arrived.reshape(n_rows, n_cols, seg_dev, 2, -1, lifted.shape[-1])
    row_ids = jnp.arange(n_rows, dtype=jnp.int32)
    cos_rows, sin_rows = turns(row_ids[:, None] * row_ids[None, :], n_rows, 1.0)
    table_rows = jnp.stack(
        [jnp.stack([cos_rows, -sin_rows], axis=1), jnp.stack([sin_rows, cos_rows], axis=1)]
    )
    values = jnp.einsum("Rarb,bcsrvu->Rcsavu", table_rows, arrived, precision=three_pass).reshape(
        2, SEGMENTS, n_rows, small
    )
    leaf_count = n_rows * small
    real_part = values[0].reshape(SEGMENTS, leaf_count)
    imag_part = values[1].reshape(SEGMENTS, leaf_count)
    zeros = jnp.zeros((DIGEST, leaf_count), jnp.float32)
    state = permute(jnp.concatenate([zeros, real_part], axis=0), hash_mds, hash_rc)
    state = state + jnp.concatenate([zeros, imag_part], axis=0)
    state = permute(state, hash_mds, hash_rc)
    return state[:DIGEST].reshape(DIGEST, n_rows, small)


def solution(mesh):
    in_specs = (
        P(None, ("rows", "cols")),
        P(None, ("rows", "cols")),
        P(),
        P(),
        P(),
        P(),
        P(("rows", "cols")),
        P(),
        P(),
    )
    out_specs = P(None, None, ("rows", "cols"))
    return jax.shard_map(
        on_device, mesh=mesh, in_specs=in_specs, out_specs=out_specs, check_vma=False
    )
```

```python
import math

import jax
import jax.numpy as jnp
from jax import lax
from jax.sharding import PartitionSpec as P

BLOWUP = 8
SEGMENTS = 8
DIGEST = 4
ROUNDS = 2


highest = lax.Precision.HIGHEST
three_pass = lax.Precision.HIGH


def from_behind(array, axis, by):
    count = lax.axis_size(axis)
    return lax.ppermute(array, axis, [(i, (i + by) % count) for i in range(count)])


def entering(value, axis):
    count, mine = (lax.axis_size(axis), lax.axis_index(axis))
    spread = jnp.broadcast_to(value, (count,))
    pieces = lax.all_to_all(spread, axis, 0, 0, tiled=True)
    earlier = jnp.arange(count, dtype=jnp.int32) < mine
    return jnp.sum(jnp.where(earlier, pieces, jnp.zeros_like(pieces)))


def squash(value):
    return value * lax.rsqrt(1.0 + value * value)


def permute(state, hash_mds, hash_rc):
    for step in range(ROUNDS):
        state = (
            jnp.dot(hash_mds, squash(state), precision=three_pass, preferred_element_type=jnp.float32)
            + hash_rc[step][:, None]
        )
    return state


def turns(product, modulus, sign):
    angle = sign * 2.0 * math.pi / modulus * (product % modulus).astype(jnp.float32)
    return (jnp.cos(angle), jnp.sin(angle))


def complex_mul(left_re, left_im, right_re, right_im):
    return (left_re * right_re - left_im * right_im, left_re * right_im + left_im * right_re)


def block_table(cos_t, sin_t):
    return jnp.concatenate(
        [jnp.concatenate([cos_t, -sin_t], axis=1), jnp.concatenate([sin_t, cos_t], axis=1)], axis=0
    )


def local_dft(values_re, values_im, sign):
    length = values_re.shape[-1]
    first = 128
    second = length // first
    leading = values_re.shape[:-1]
    stacked = jnp.concatenate(
        [values_re.reshape(leading + (first, second)), values_im.reshape(leading + (first, second))],
        axis=-2,
    )
    index_one = jnp.arange(first, dtype=jnp.int32)
    index_two = jnp.arange(second, dtype=jnp.int32)
    table_one = block_table(*turns(index_one[:, None] * index_one[None, :], first, sign))
    section = jnp.einsum("kn,...nm->...km", table_one, stacked, precision=three_pass)
    section_re, section_im = section[..., :first, :], section[..., first:, :]
    twist_cos, twist_sin = turns(index_one[:, None] * index_two[None, :], length, sign)
    section_re, section_im = complex_mul(section_re, section_im, twist_cos, twist_sin)
    table_two = block_table(*turns(index_two[:, None] * index_two[None, :], second, sign))
    both = jnp.concatenate([section_re, section_im], axis=-1)
    final = jnp.einsum("jn,...kn->...jk", table_two, both, precision=three_pass)
    final_re = final[..., :second, :].reshape(leading + (length,))
    final_im = final[..., second:, :].reshape(leading + (length,))
    return (final_re, final_im)


def lift_dft(values_re, values_im, sign):
    segs, phases, length = values_re.shape
    first = 128
    second = length // first
    stacked = jnp.concatenate(
        [values_re.reshape(segs, phases, first, second), values_im.reshape(segs, phases, first, second)],
        axis=2,
    )
    index_one = jnp.arange(first, dtype=jnp.int32)
    index_two = jnp.arange(second, dtype=jnp.int32)
    table_one = block_table(*turns(index_one[:, None] * index_one[None, :], first, sign))
    section = jnp.einsum("kn,spnm->skpm", table_one, stacked, precision=three_pass)
    section_re, section_im = section[:, :first], section[:, first:]
    twist_cos, twist_sin = turns(index_one[:, None] * index_two[None, :], length, sign)
    section_re, section_im = complex_mul(
        section_re, section_im, twist_cos[:, None, :], twist_sin[:, None, :]
    )
    both = jnp.concatenate([section_re, section_im], axis=-1).reshape(segs, first * phases, 2 * second)
    table_two = block_table(*turns(index_two[:, None] * index_two[None, :], second, sign))
    final = jnp.einsum("jm,sxm->sjx", table_two, both, precision=three_pass)
    final_re = final[:, :second].reshape(segs, length * phases)
    final_im = final[:, second:].reshape(segs, length * phases)
    return (final_re, final_im)


def lift_eval(coef_re, coef_im, phases, row_index, total_rows, devices):
    segs, length = coef_re.shape
    first = 128
    second = length // first
    band = length * phases
    stacked = jnp.concatenate(
        [coef_re.reshape(segs, first, second), coef_im.reshape(segs, first, second)], axis=1
    )
    index_one = jnp.arange(first, dtype=jnp.int32)
    index_two = jnp.arange(second, dtype=jnp.int32)
    index_p = jnp.arange(phases, dtype=jnp.int32)
    k_one = index_one[None, :, None]
    n_one = index_one[None, None, :]
    p_one = index_p[:, None, None]
    angle_one = (
        (k_one * n_one % first) * (total_rows // first)
        + (p_one * n_one) * (total_rows // (first * phases))
        + (phases * k_one + p_one) * row_index
    )
    cos_one, sin_one = turns(angle_one, total_rows, 1.0)
    table_one = jnp.concatenate(
        [jnp.concatenate([cos_one, -sin_one], axis=2), jnp.concatenate([sin_one, cos_one], axis=2)],
        axis=1,
    )
    section = jnp.einsum("pkn,snm->skpm", table_one, stacked, precision=three_pass)
    section_re, section_im = section[:, :first], section[:, first:]
    twist = (phases * index_one[:, None, None] + index_p[None, :, None]) * index_two[None, None, :]
    twist_cos, twist_sin = turns(twist, band, 1.0)
    section_re, section_im = complex_mul(section_re, section_im, twist_cos, twist_sin)
    both = jnp.concatenate([section_re, section_im], axis=-1).reshape(segs, first * phases, 2 * second)
    angle_two = (index_two[:, None] * index_two[None, :] % second) * (total_rows // second) + (
        index_two[:, None] * row_index * (first * phases)
    )
    cos_two, sin_two = turns(angle_two, total_rows, 1.0)
    rows_per = 2 * second // devices
    table_two = (
        jnp.stack(
            [jnp.concatenate([cos_two, -sin_two], axis=1), jnp.concatenate([sin_two, cos_two], axis=1)]
        )
        .reshape(2, devices, rows_per // 2, 2 * second)
        .transpose(1, 0, 2, 3)
        .reshape(2 * second, 2 * second)
    )
    final = jnp.einsum("jm,sxm->sjx", table_two, both, precision=three_pass)
    return final.reshape(segs, devices, rows_per, first * phases).transpose(1, 0, 2, 3)


def regroup(values):
    return lax.all_to_all(values, ("rows", "cols"), split_axis=1, concat_axis=1, tiled=True)


def column_relay(values):
    return lax.all_to_all(values, "cols", split_axis=1, concat_axis=1, tiled=True)


def on_device(trace, selectors, mds, quad, alpha, challenges, divisor_inv, hash_mds, hash_rc):
    width = trace.shape[0]
    rows_dev = trace.shape[1]
    n_rows = lax.axis_size("rows")
    n_cols = lax.axis_size("cols")
    devices = n_rows * n_cols
    total_rows = rows_dev * devices
    flat_index = lax.axis_index(("rows", "cols"))
    row_index = lax.axis_index("rows")
    rim = from_behind(trace[:, :BLOWUP], ("rows", "cols"), -1)
    extended = jnp.concatenate([trace, rim], axis=1)
    following = extended[:, BLOWUP:]
    linear = jnp.dot(mds, trace, precision=three_pass, preferred_element_type=jnp.float32)
    cons = following - linear - quad[:, None] * trace * trace
    step_size = challenges[0] / jnp.sqrt(jnp.float32(total_rows))
    gamma = challenges[1]
    numer = 1.0 + step_size * (extended[0] + gamma * extended[1])
    denom = 1.0 + step_size * (extended[2] + gamma * extended[3])
    ratio_log = jnp.log(numer) - jnp.log(denom)
    own_terms = ratio_log[:rows_dev]
    running_sum = jnp.cumsum(own_terms)
    offset = entering(running_sum[-1], ("rows", "cols"))
    running = jnp.exp(offset + running_sum - own_terms)
    window = own_terms
    for shift_step in range(1, BLOWUP):
        window = window + ratio_log[shift_step : shift_step + rows_dev]
    grand = running * (jnp.exp(window) * denom[:rows_dev] - numer[:rows_dev]) / step_size
    picked = selectors.astype(jnp.float32)
    combined = (
        jnp.sum(alpha[:width, None] * picked[:width] * cons, axis=0)
        + alpha[width] * picked[width] * grand
    )
    quotient = divisor_inv * combined
    parts = rows_dev // devices
    gathered = regroup(quotient.reshape(1, rows_dev)).reshape(devices, parts)
    block_index = jnp.arange(devices, dtype=jnp.int32)
    cos_block, sin_block = turns(block_index[:, None] * block_index[None, :], devices, -1.0)
    first_re = jnp.dot(cos_block, gathered, precision=three_pass, preferred_element_type=jnp.float32)
    first_im = jnp.dot(sin_block, gathered, precision=three_pass, preferred_element_type=jnp.float32)
    global_pos = flat_index * parts + jnp.arange(parts, dtype=jnp.int32)
    twist_cos, twist_sin = turns(block_index[:, None] * global_pos[None, :], total_rows, -1.0)
    first_re, first_im = complex_mul(first_re, first_im, twist_cos, twist_sin)
    ordered = (
        jnp.stack([first_re, first_im])
        .reshape(2, n_cols, n_rows, parts)
        .transpose(0, 2, 1, 3)
        .reshape(2, devices * parts)
    )
    columns = regroup(ordered)
    coef_re, coef_im = local_dft(columns[0], columns[1], -1.0)
    coef_re = coef_re / total_rows
    coef_im = coef_im / total_rows
    seg_dev = SEGMENTS // n_cols
    seg_rows = rows_dev // SEGMENTS
    packed = jnp.stack([coef_re, coef_im]).reshape(2, n_cols, seg_dev, seg_rows)
    owned = column_relay(packed)
    owned = owned.transpose(0, 2, 3, 1).reshape(2, seg_dev, seg_rows * n_cols)
    short = seg_rows * n_cols
    band = short * SEGMENTS
    small = band // devices
    lifted = lift_eval(owned[0], owned[1], SEGMENTS, row_index, total_rows, devices)
    arrived = lax.all_to_all(lifted, ("rows", "cols"), 0, 0, tiled=True)
    arrived = arrived.reshape(n_rows, n_cols, seg_dev, 2, -1, lifted.shape[-1])
    row_ids = jnp.arange(n_rows, dtype=jnp.int32)
    cos_rows, sin_rows = turns(row_ids[:, None] * row_ids[None, :], n_rows, 1.0)
    table_rows = jnp.stack(
        [jnp.stack([cos_rows, -sin_rows], axis=1), jnp.stack([sin_rows, cos_rows], axis=1)]
    )
    values = jnp.einsum("Rarb,bcsrvu->Rcsavu", table_rows, arrived, precision=three_pass).reshape(
        2, SEGMENTS, n_rows, small
    )
    leaf_count = n_rows * small
    real_part = values[0].reshape(SEGMENTS, leaf_count)
    imag_part = values[1].reshape(SEGMENTS, leaf_count)
    zeros = jnp.zeros((DIGEST, leaf_count), jnp.float32)
    state = permute(jnp.concatenate([zeros, real_part], axis=0), hash_mds, hash_rc)
    state = state + jnp.concatenate([zeros, imag_part], axis=0)
    state = permute(state, hash_mds, hash_rc)
    return state[:DIGEST].reshape(DIGEST, n_rows, small)


def solution(mesh):
    in_specs = (
        P(None, ("rows", "cols")),
        P(None, ("rows", "cols")),
        P(),
        P(),
        P(),
        P(),
        P(("rows", "cols")),
        P(),
        P(),
    )
    out_specs = P(None, None, ("rows", "cols"))
    return jax.shard_map(
        on_device, mesh=mesh, in_specs=in_specs, out_specs=out_specs, check_vma=False
    )
```
